32 devices in a mesh: leaf: 32 (over z, y, x, core).
Axes of the slice: x: 2, y: 2, z: 4, core: 2. Of those that a mesh axis runs over, the one named last changes fastest.
Arguments:
- near_blocks: bfloat16 [64, 26, 256, 256], P('leaf'), may hold values from -0.0582 to 0.0582
- diag_blocks: bfloat16 [64, 256, 256], P('leaf'), as said below
- bases: bfloat16 [64, 256, 256], P('leaf'), as said below
- leaf_nbrs: int32 [64, 26], P('leaf'), may hold values from -1 to 63, as said below
- parent_nbrs: int32 [8, 5], replicated, may hold values from 0 to 7, as said below
Outputs:
- leaf_factor: float32 [64, 128, 128], P('leaf')
- leaf_panel: float32 [64, 128, 128], P('leaf')
- merged: float32 [64, 5, 128, 1024], P('leaf')
- parent_block: float32 [8192, 1024], P('leaf')
The draws below stay inside these ranges and needn't reach their ends.
Inputs may be any that keep to these rules, and one draw needn't show every extreme that they name: `leaf_nbrs`: row i lists distinct leaves j with j != i and |j - i| <= 16; live entries come first and -1 fills the rest; every row has at least 13 live entries and some row has all 26. `parent_nbrs`: row P begins with P itself, followed by the other 4 parents nearest to P in numbering, distinct, equally near ones in any order. `diag_blocks`: each block is symmetric positive definite. `bases`: each basis is an orthogonal matrix rounded to bfloat16.
All inputs are finite; a program needn't handle non-finite values.
Results may differ from the reference program's by a relative error of at most 0.001.
The reference program's roundings to bfloat16 on the way count: a program that leaves them out, or rounds other values in their place, can miss the bound.
Values may be sent and summed in bfloat16 or wider, within the bound.
A program may use at most 128 MiB of HBM per device.

```python
import jax
import jax.numpy as jnp
from jax import lax

LR = 256
RANK = 128
NB = 26
REACH = 16
CHILDREN = 8
LEAVES = 64
PARENTS = 8
PNB = 5


def draw_near_blocks(key, part):
    base_key = jax.random.fold_in(key, 53)

    def one_leaf(leaf_index):
        leaf_key = jax.random.fold_in(base_key, leaf_index)
        values = jnp.clip(0.013 * jax.random.normal(leaf_key, (NB, LR, LR), jnp.float32), -0.058, 0.058)
        return values.astype(jnp.bfloat16)
    return lax.map(one_leaf, jnp.arange(LEAVES, dtype=jnp.int32))


def draw_diag_blocks(key, part):
    key_scale, key_mix = jax.random.split(jax.random.fold_in(key, 11))
    scales = jnp.exp(jax.random.uniform(key_scale, (LEAVES, LR), jnp.float32, jnp.log(1.0), jnp.log(4.0)))

    def one_leaf(leaf_index):
        leaf_key = jax.random.fold_in(key_mix, leaf_index)
        mixing = jax.random.normal(leaf_key, (LR, LR), jnp.float32)
        gram = jnp.dot(mixing, mixing.T, precision=lax.Precision.HIGHEST) / LR
        return 0.5 * (gram + gram.T)
    grams = lax.map(one_leaf, jnp.arange(LEAVES, dtype=jnp.int32))
    blocks = grams + scales[:, :, None] * jnp.eye(LR, dtype=jnp.float32)[None]
    return blocks.astype(jnp.bfloat16)


def draw_bases(key, part):
    source = jax.random.normal(jax.random.fold_in(key, 23), (LEAVES, LR, LR), jnp.float32)
    orthogonal, upper_part = jnp.linalg.qr(source)
    return orthogonal.astype(jnp.bfloat16)


def draw_leaf_nbrs(key, part):
    base_key = jax.random.fold_in(key, 37)
    key_rank, key_count, key_full = jax.random.split(base_key, 3)
    offsets = jnp.concatenate([jnp.arange(-REACH, 0), jnp.arange(1, REACH + 1)]).astype(jnp.int32)
    row_keys = jax.random.split(key_rank, LEAVES)
    row_ranks = jax.vmap(lambda row_key: jax.random.permutation(row_key, 2 * REACH))(row_keys).astype(jnp.int32)
    leaves = jnp.arange(LEAVES, dtype=jnp.int32)
    targets = leaves[:, None] + offsets[None, :]
    in_range = (targets >= 0) & (targets < LEAVES)
    scores = in_range.astype(jnp.int32) * 1024 + row_ranks
    top_scores, picked_slots = lax.top_k(scores, NB)
    chosen = leaves[:, None] + offsets[picked_slots]
    counts = jax.random.randint(key_count, (LEAVES,), 13, NB + 1)
    full_leaf = jax.random.randint(key_full, (), REACH, LEAVES - REACH)
    counts = jnp.where(leaves == full_leaf, NB, counts)
    slot_ids = jnp.arange(NB, dtype=jnp.int32)[None, :]
    is_live = (slot_ids < counts[:, None]) & (top_scores >= 1024)
    return jnp.where(is_live, chosen, -1).astype(jnp.int32)


def draw_parent_nbrs(key, part):
    row_ranks = jax.random.permutation(jax.random.fold_in(key, 41), PARENTS).astype(jnp.int32)
    parents = jnp.arange(PARENTS, dtype=jnp.int32)
    distance = jnp.abs(parents[:, None] - parents[None, :])
    scores = -distance * 4096 + row_ranks[None, :]
    top_scores, picked = lax.top_k(scores, PNB)
    return picked.astype(jnp.int32)


def setup_inputs(seed: int = 0) -> dict:
    key_of = jax.random.split(jax.random.key(seed), 6)
    near_blocks = draw_near_blocks(jax.random.fold_in(key_of[5], 71), 0)
    diag_blocks = draw_diag_blocks(jax.random.fold_in(key_of[5], 71), 0)
    bases = draw_bases(jax.random.fold_in(key_of[5], 71), 0)
    leaf_nbrs = draw_leaf_nbrs(jax.random.fold_in(key_of[5], 71), 0)
    parent_nbrs = draw_parent_nbrs(jax.random.fold_in(key_of[5], 71), 0)
    return dict(near_blocks=near_blocks, diag_blocks=diag_blocks, bases=bases, leaf_nbrs=leaf_nbrs, parent_nbrs=parent_nbrs)


highest = lax.Precision.HIGHEST

def lower_solve(lower_factor, right_side):
    return lax.linalg.triangular_solve(lower_factor, right_side, left_side=True, lower=True)

def back_solve(lower_factor, right_side):
    return lax.linalg.triangular_solve(lower_factor, right_side, left_side=True, lower=True, transpose_a=True)

def factor_leaf(block, basis):
    basis_wide = basis.astype(jnp.float32)
    half_proj = jnp.dot(basis_wide.T, block.astype(jnp.float32), precision=highest).astype(jnp.bfloat16)
    half_proj = lax.optimization_barrier(half_proj).astype(jnp.float32)
    dense = jnp.dot(half_proj, basis_wide, precision=highest)
    redundant = LR - RANK
    lower_factor = jnp.linalg.cholesky(dense[:redundant, :redundant])
    panel_rows = lower_solve(lower_factor, dense[:redundant, redundant:])
    skeleton = dense[redundant:, redundant:] - jnp.dot(panel_rows.T, panel_rows, precision=highest)
    shift_rows = back_solve(lower_factor, panel_rows)
    return (lower_factor, panel_rows, skeleton, shift_rows)

def reference(near_blocks, diag_blocks, bases, leaf_nbrs, parent_nbrs):
    redundant = LR - RANK
    leaf_factor, leaf_panel, skeleton, shift_wide = jax.vmap(factor_leaf)(diag_blocks, bases)
    leaf_shift = lax.optimization_barrier(shift_wide.astype(jnp.bfloat16)).astype(jnp.float32)

    def leaf_row(leaf_index):
        neighbours = leaf_nbrs[leaf_index]
        is_live = neighbours >= 0
        clipped = jnp.maximum(neighbours, 0)
        basis_wide = bases[leaf_index].astype(jnp.float32)
        half_proj = jnp.einsum('ba,nbc->nac', basis_wide, near_blocks[leaf_index].astype(jnp.float32), precision=highest).astype(jnp.bfloat16)
        half_proj = lax.optimization_barrier(half_proj).astype(jnp.float32)
        coupled = jnp.einsum('nac,ncb->nab', half_proj, bases[clipped].astype(jnp.float32), precision=highest)
        own_shift = leaf_shift[leaf_index]
        first_term = jnp.einsum('ka,nkb->nab', own_shift, coupled[:, :redundant, redundant:], precision=highest)
        second_term = jnp.einsum('nak,nkb->nab', coupled[:, redundant:, :redundant], leaf_shift[clipped], precision=highest)
        near_schur = jnp.where(is_live[:, None, None], coupled[:, redundant:, redundant:] - first_term - second_term, jnp.float32(0.0))
        parent = leaf_index // CHILDREN
        position = leaf_index % CHILDREN
        targets = parent_nbrs[parent]
        children = jnp.arange(CHILDREN, dtype=jnp.int32)
        slot_hits = is_live[None, None, :] & (clipped[None, None, :] // CHILDREN == targets[:, None, None]) & (clipped[None, None, :] % CHILDREN == children[None, :, None])
        self_hit = (targets[:, None] == parent) & (children[None, :] == position)
        parent_rows = jnp.einsum('qbn,nxy->qxby', slot_hits.astype(jnp.float32), near_schur, precision=highest)
        parent_rows = parent_rows + self_hit.astype(jnp.float32)[:, None, :, None] * skeleton[leaf_index][None, :, None, :]
        parent_rows = parent_rows.reshape(PNB, RANK, CHILDREN * RANK)
        return (parent_rows, parent_rows[0])
    merged, diagonal_rows = lax.map(leaf_row, jnp.arange(LEAVES, dtype=jnp.int32))
    blocks = diagonal_rows.reshape(PARENTS, CHILDREN * RANK, CHILDREN * RANK)
    symmetric = 0.5 * (blocks + jnp.transpose(blocks, (0, 2, 1)))
    return (leaf_factor, leaf_panel, merged, symmetric.reshape(LEAVES * RANK, CHILDREN * RANK))
```

```python
import functools

import jax
import jax.numpy as jnp
from jax import lax
from jax.experimental import pallas as pl
from jax.experimental.pallas import tpu as pltpu
from jax.sharding import PartitionSpec as P

RANK = 128
REACH = 16
CHILDREN = 8
PANEL = 32
PLANE = 4
LINKS = ("x", "y", "up", "down")
MESH = pl.DeviceIdType.MESH
highest = lax.Precision.HIGHEST


def matmul(a, b):
    return jnp.dot(a, b, preferred_element_type=jnp.float32)


def matmul_t(a, b, precision=None):
    return lax.dot_general(
        a, b, (((0,), (0,)), ((), ())), preferred_element_type=jnp.float32, precision=precision
    )


def plan():
    def both(plane, chip):
        return [(plane, chip, 0), (plane, chip, 1)]

    inbound = (
        {
            "x": both(0, 1) + [(0, 3, 0)] + both(-1, 1),
            "y": both(0, 2) + [(0, 3, 1)] + both(-1, 2),
            "up": both(-1, 0) + both(-1, 3),
            "down": both(1, 0),
        },
        {
            "x": both(0, 0) + both(0, 2),
            "y": both(0, 3) + both(-1, 3),
            "up": both(-1, 1) + both(-1, 2),
            "down": both(1, 1) + both(1, 0),
        },
        {
            "x": both(0, 3) + both(0, 1),
            "y": both(0, 0) + both(1, 0),
            "up": both(-1, 2) + both(-1, 3),
            "down": both(1, 2) + both(1, 1),
        },
        {
            "x": both(0, 2) + [(0, 0, 0)] + both(1, 2),
            "y": both(0, 1) + [(0, 0, 1)] + both(1, 1),
            "up": both(-1, 3),
            "down": both(1, 3) + both(1, 0),
        },
    )
    outbound = []
    for place in range(PLANE):
        out = {"x": inbound[place ^ 1]["x"], "y": inbound[place ^ 2]["y"]}
        out["up"] = [(plane + 1, chip, leaf) for plane, chip, leaf in inbound[place]["up"]]
        out["down"] = [(plane - 1, chip, leaf) for plane, chip, leaf in inbound[place]["down"]]
        outbound.append(out)
    held = [{(0, place, leaf): 0 for leaf in range(2)} for place in range(PLANE)]
    arrivals = [[] for _ in range(PLANE)]
    queue = {(place, link): 0 for place in range(PLANE) for link in LINKS}
    now = 0
    while any(queue[place, link] < len(outbound[place][link]) for place, link in queue):
        now += 1
        landed = []
        for (place, link), done in queue.items():
            items = outbound[place][link]
            if done < len(items) and held[place].get(items[done], now) < now:
                target = {"x": place ^ 1, "y": place ^ 2}.get(link, place)
                landed.append((target, inbound[target][link][done]))
                queue[place, link] = done + 1
        for target, item in landed:
            held[target][item] = now
            arrivals[target].append((now, item))
    return outbound, arrivals


OUTBOUND, ARRIVALS = plan()
STEPS = max(now for events in ARRIVALS for now, _ in events)


def shift_of(place, item):
    plane, chip, _ = item
    return PLANE * plane + chip - place


def chunk_order(place):
    ready = {0: 0}
    for now, item in ARRIVALS[place]:
        ready[shift_of(place, item)] = now
    first = (0, (place ^ 1) - place)
    rest = sorted((now, delta) for delta, now in ready.items() if delta not in first)
    return list(first) + [delta for _, delta in rest], [ready[first[1]]] + [now for now, _ in rest]


def eliminate(diag, bases, factor, panel, skeleton, shift, bases_t, work, rows, prepare, serve):
    per_device, leaf_rows = bases.shape[0], bases.shape[1]
    red = leaf_rows - RANK
    wide = 2 * red + RANK
    row_id = lax.broadcasted_iota(jnp.int32, (red, red), 0)
    col_id = lax.broadcasted_iota(jnp.int32, (red, red), 1)
    low_corner = []
    for leaf in range(per_device):
        basis = bases[leaf]
        basis_t = basis.T
        bases_t[leaf] = basis_t
        half = matmul(basis_t, diag[leaf]).astype(jnp.bfloat16)
        dense = matmul(half, basis)
        top = dense[:red, :red]
        work[leaf, :, :red] = 0.5 * (top + top.T)
        work[leaf, :, red : red + RANK] = dense[:red, red:]
        work[leaf, :, red + RANK :] = (row_id == col_id).astype(jnp.float32)
        low_corner.append(dense[red:, red:])
    prepare()
    sub = lax.broadcasted_iota(jnp.int32, (PANEL, 1), 0)
    for start in range(0, red, PANEL):
        strips = [work[leaf, start : start + PANEL, :] for leaf in range(per_device)]
        for k in range(PANEL):
            for leaf in range(per_device):
                strip = strips[leaf]
                column = strip[:, start + k : start + k + 1]
                ratio = jnp.where(sub > k, column / column[k : k + 1], 0.0)
                strips[leaf] = strip - ratio * strip[k : k + 1, :]
        lane = lax.broadcasted_iota(jnp.int32, (PANEL, wide), 1)
        line = lax.broadcasted_iota(jnp.int32, (PANEL, wide), 0)
        for leaf in range(per_device):
            strip = strips[leaf]
            pivots = jnp.sum(jnp.where(lane == line + start, strip, 0.0), axis=1, keepdims=True)
            strip = strip * (1.0 / jnp.sqrt(pivots))
            rows[leaf, start : start + PANEL, :] = strip
            if start + PANEL < red:
                work[leaf] = work[leaf] - matmul_t(strip[:, :red], strip, highest)
        serve(start + PANEL)
    for leaf in range(per_device):
        solved = rows[leaf, :, red : red + RANK]
        inverse = jnp.where(col_id <= row_id, rows[leaf, :, red + RANK :], 0.0)
        shift[leaf] = matmul_t(inverse, solved, highest).astype(jnp.bfloat16)
    serve(red + 1)
    for leaf in range(per_device):
        solved = rows[leaf, :, red : red + RANK]
        panel[leaf] = solved
        skeleton[leaf] = low_corner[leaf] - matmul_t(solved, solved, highest)
        upper = jnp.where(col_id >= row_id, rows[leaf, :, :red], 0.0)
        factor[leaf] = upper.T


def split(values):
    high = values.astype(jnp.bfloat16)
    return high, (values - high.astype(jnp.float32)).astype(jnp.bfloat16)


def level_kernel(
    count,
    parents,
    targets,
    nbrs,
    diag,
    bases,
    near,
    factor,
    panel,
    blocks,
    landed,
    win_bases,
    win_shift,
    shift,
    skeleton,
    bases_t,
    work,
    rows,
    near_in,
    sides,
    diagonal,
    send,
    recv,
    pass_send,
    pass_recv,
    own_sem,
    near_sem,
    row_send,
    row_recv,
    found,
    lookup,
    found_sem,
):
    per_device, slots = near_in.shape[0], near_in.shape[1]
    red = shift.shape[1]
    total = count // 2
    me = lax.axis_index("leaf")
    core, chip = me % 2, me // 2
    sibling = me + 1 - 2 * core
    place = chip % PLANE
    size = CHILDREN // per_device
    seat = me % size
    across = me + 2 * (1 - 2 * (place % 2))
    along = me + 4 * (1 - 2 * (place // 2))
    device = {"x": across, "y": along, "up": me + 2 * PLANE, "down": me - 2 * PLANE}
    present = {"up": chip + PLANE < total, "down": chip - PLANE >= 0}
    far = across + 1 - 2 * core

    fetches = [
        pltpu.make_async_copy(near.at[leaf], near_in.at[leaf], near_sem.at[leaf])
        for leaf in range(per_device)
    ]
    for fetch in fetches:
        fetch.start()

    barrier = pltpu.get_barrier_semaphore()
    for other in (sibling, across, along, far):
        pl.semaphore_signal(barrier, inc=1, device_id=(other,), device_id_type=MESH)
    peers = jnp.int32(4)
    for link in ("up", "down"):

        @pl.when(present[link])
        def _(link=link):
            pl.semaphore_signal(barrier, inc=1, device_id=(device[link],), device_id_type=MESH)

        peers = peers + present[link].astype(jnp.int32)

    pairs = ((bases, win_bases), (shift, win_shift))

    def exists(delta):
        return (chip + delta >= 0) & (chip + delta < total)

    def slot_of(delta, holder):
        return 2 * (PLANE + delta) + holder

    def hop(kind, at, link, order):
        item = OUTBOUND[at][link][order]
        delta = shift_of(at, item)
        moved = {"x": at - (at ^ 1), "y": at - (at ^ 2), "up": -PLANE, "down": PLANE}[link]
        source, window = pairs[kind]
        leaf = item[2]
        return pltpu.make_async_remote_copy(
            src_ref=source.at[leaf] if delta == 0 else window.at[slot_of(delta, core), leaf],
            dst_ref=window.at[slot_of(delta + moved, core), leaf],
            send_sem=send.at[kind, LINKS.index(link), order],
            recv_sem=recv.at[kind, PLANE + delta + moved, leaf],
            device_id=(device[link],),
            device_id_type=MESH,
        )

    def arrival(kind, delta, leaf):
        window = pairs[kind][1]
        there = window.at[slot_of(delta, core), leaf]
        return pltpu.make_async_remote_copy(
            src_ref=there,
            dst_ref=there,
            send_sem=send.at[kind, 0, 0],
            recv_sem=recv.at[kind, PLANE + delta, leaf],
            device_id=(sibling,),
            device_id_type=MESH,
        )

    def relay(kind, delta, leaf, own=False):
        source, window = pairs[kind]
        there = window.at[slot_of(delta, core), leaf]
        return pltpu.make_async_remote_copy(
            src_ref=source.at[leaf] if own else there,
            dst_ref=there,
            send_sem=pass_send.at[kind, PLANE + delta, leaf],
            recv_sem=pass_recv.at[kind, PLANE + delta, leaf],
            device_id=(sibling,),
            device_id_type=MESH,
        )

    def relayed(kind, delta, leaf):
        window = pairs[kind][1]
        there = window.at[slot_of(delta, 1 - core), leaf]
        return pltpu.make_async_remote_copy(
            src_ref=there,
            dst_ref=there,
            send_sem=pass_send.at[kind, PLANE + delta, leaf],
            recv_sem=pass_recv.at[kind, PLANE + delta, leaf],
            device_id=(sibling,),
            device_id_type=MESH,
        )

    def on_links(kind, at, item, act):
        for link in LINKS:
            for order, entry in enumerate(OUTBOUND[at][link]):
                if entry == item:
                    if link in present:
                        pl.when(present[link])(lambda: act(hop(kind, at, link, order)))
                    else:
                        act(hop(kind, at, link, order))

    def start(copy):
        copy.start()

    def stop(copy):
        copy.wait_send()

    def own_copy(kind):
        source, window = pairs[kind]
        return pltpu.make_async_copy(source, window.at[slot_of(0, core)], own_sem.at[kind])

    def by_place(act):
        for at in range(PLANE):
            pl.when(place == at)(lambda: act(at))

    def dispatch(kind):
        def act(at):
            for leaf in range(per_device):
                on_links(kind, at, (0, at, leaf), start)

        by_place(act)
        for leaf in range(per_device):
            relay(kind, 0, leaf, own=True).start()
        own_copy(kind).start()

    def serve(kind, step):
        def act(at):
            for now, item in ARRIVALS[at]:
                if now == step:
                    delta, leaf = shift_of(at, item), item[2]

                    def one():
                        arrival(kind, delta, leaf).wait_recv()
                        on_links(kind, at, item, start)
                        relay(kind, delta, leaf).start()

                    if item[0] == 0:
                        one()
                    else:
                        pl.when(exists(delta))(one)

        by_place(act)

    def finish(kind):
        def act(at):
            for leaf in range(per_device):
                on_links(kind, at, (0, at, leaf), stop)
            for _, item in ARRIVALS[at]:
                delta, leaf = shift_of(at, item), item[2]

                def one():
                    on_links(kind, at, item, stop)
                    relay(kind, delta, leaf).wait_send()

                if item[0] == 0:
                    one()
                else:
                    pl.when(exists(delta))(one)

        by_place(act)
        for leaf in range(per_device):
            relay(kind, 0, leaf, own=True).wait_send()

    number = me * per_device
    parent = number // CHILDREN
    low = jnp.clip(parent - targets // 2, 0, parents - targets)
    home = parent - low
    blocks[...] = jnp.zeros_like(blocks)
    reach = found.shape[1]
    offset = lax.broadcasted_iota(jnp.int32, (reach, slots), 0) - reach // 2
    order = lax.broadcasted_iota(jnp.int32, (reach, slots), 1)
    for leaf in range(per_device):
        away = offset + number + leaf
        hit = (nbrs[leaf : leaf + 1, :] == away) & (away >= 0)
        slot = jnp.max(jnp.where(hit, order, -1), axis=1, keepdims=True)
        found[leaf] = jnp.broadcast_to(slot, found.shape[1:])
    table = pltpu.make_async_copy(found, lookup, found_sem)
    table.start()

    def prepare():
        pl.semaphore_wait(barrier, peers)
        dispatch(0)

    def between(point):
        panels = red // PANEL
        if point <= red:
            serve(0, point // PANEL)
        else:
            dispatch(1)

    eliminate(diag, bases, factor, panel, skeleton, shift, bases_t, work, rows, prepare, between)
    for step in range(red // PANEL + 1, STEPS + 1):
        serve(0, step)
    for fetch in fetches:
        fetch.wait()

    unroll = max(n for n in range(1, 14) if slots % n == 0)

    @pl.loop(0, slots // unroll)
    def _(turn):
        for k in range(unroll):
            n = turn * unroll + k
            for leaf in range(per_device):
                half = matmul(bases_t[leaf], near_in[leaf, n]).astype(jnp.bfloat16)
                high, low_part = split(-matmul_t(shift[leaf], half[:red]))
                sides[leaf, n, :, : 2 * RANK] = half[red:]
                sides[leaf, n, :, 2 * RANK : 4 * RANK] = high
                sides[leaf, n, :, 4 * RANK :] = low_part

    table.wait()
    own_copy(0).wait()
    own_copy(1).wait()

    orders = [chunk_order(at) for at in range(PLANE)]

    def pick(values):
        chosen = jnp.int32(values[0])
        for at in range(1, PLANE):
            chosen = jnp.where(place == at, jnp.int32(values[at]), chosen)
        return chosen

    def couple(delta):
        for kind in range(2):
            for leaf in range(per_device):
                relayed(kind, delta, leaf).wait_recv()
        for holder in range(2):
            for leaf in range(per_device):
                slot = slot_of(delta, holder)
                basis = win_bases[slot, leaf]
                moved = win_shift[slot, leaf]
                outer = basis[:, red:]
                change = outer.astype(jnp.float32) - matmul(basis[:, :red], moved)
                high, low_part = split(change)
                right = jnp.concatenate([high, low_part, outer, outer], axis=0)
                other = ((chip + delta) * 2 + holder) * per_device + leaf
                left = []
                live = []
                for mine in range(per_device):
                    n = lookup[mine, other - number - mine + REACH + CHILDREN, 0]
                    side = sides[mine, jnp.maximum(n, 0)]
                    left.append(jnp.concatenate([side[:, : 2 * RANK], side], axis=1))
                    live.append(n >= 0)
                schur = matmul(jnp.concatenate(left, axis=0), right)
                column = pl.multiple_of((other % CHILDREN) * RANK, RANK)
                row = other // CHILDREN - low
                for mine in range(per_device):
                    apart = other - number - mine
                    value = jnp.where(live[mine], schur[mine * RANK : (mine + 1) * RANK], 0.0)

                    @pl.when((apart <= REACH) & (apart >= -REACH))
                    def _(mine=mine, value=value):
                        blocks[mine, row, :, pl.ds(column, RANK)] = value

    def row_copy(t):
        other = (seat + t) % size
        width = per_device * RANK
        return pltpu.make_async_remote_copy(
            src_ref=diagonal.at[:, :, pl.ds(pl.multiple_of(other * width, 128), width)],
            dst_ref=landed.at[size - t],
            send_sem=row_send.at[t],
            recv_sem=row_recv.at[size - t],
            device_id=(me - seat + other,),
            device_id_type=MESH,
        )

    served = 0
    chunks = len(orders[0][0])
    for turn in range(chunks):
        if turn:
            needed = max(order[1][turn - 1] for order in orders)
            while served < needed:
                served += 1
                serve(1, served)
        delta = pick([order[0][turn] for order in orders])
        pl.when(exists(delta))(lambda: couple(delta))
        if turn == 0:
            for leaf in range(per_device):
                column = pl.multiple_of(((number + leaf) % CHILDREN) * RANK, RANK)
                blocks[leaf, home, :, pl.ds(column, RANK)] = skeleton[leaf]
        if turn == 1:
            for leaf in range(per_device):
                diagonal[leaf] = blocks[leaf, home].astype(jnp.bfloat16)
            for t in range(1, size):
                row_copy(t).start()

    finish(0)
    finish(1)
    for t in range(1, size):
        row_copy(size - t).wait_recv()
    for t in range(1, size):
        row_copy(t).wait_send()


def place_kernel(
    parents, factor, panel, blocks, landed, factor_out, panel_out, merged, block_out, block, sems
):
    per_device, targets = blocks.shape[0], blocks.shape[1]
    size = landed.shape[0]
    width = per_device * RANK
    me = lax.axis_index("leaf")
    seat = me % size
    parent = me * per_device // CHILDREN
    low = jnp.clip(parent - targets // 2, 0, parents.shape[0] - targets)
    copies = []

    def put(source, target):
        copy = pltpu.make_async_copy(source, target, sems.at[len(copies)])
        copy.start()
        copies.append(copy)

    for q in range(targets):
        row = parents[parent, q] - low
        for leaf in range(per_device):
            put(blocks.at[leaf, row], merged.at[leaf, q])
    put(factor, factor_out)
    put(panel, panel_out)
    for t in range(size):
        columns = pl.ds(pl.multiple_of(((seat + t) % size) * width, 128), width)
        mine = blocks[:, parent - low, :, columns].reshape(width, width)
        if t == 0:
            theirs = mine
        else:
            theirs = landed[t].reshape(width, width).astype(jnp.float32)
        block[:, columns] = 0.5 * (mine + theirs.T)
        put(block.at[:, columns], block_out.at[:, columns])
    for copy in copies:
        copy.wait()


def local(count, near_blocks, diag_blocks, bases, leaf_nbrs, parent_nbrs):
    per_device, leaf_rows = bases.shape[0], bases.shape[1]
    red = leaf_rows - RANK
    slots = near_blocks.shape[1]
    parents, targets = parent_nbrs.shape
    assert per_device == 2 and REACH == 4 * PLANE
    vmem = pl.BlockSpec(memory_space=pltpu.VMEM)
    smem = pl.BlockSpec(memory_space=pltpu.SMEM)
    hbm = pl.BlockSpec(memory_space=pltpu.HBM)
    f32, bf16 = jnp.float32, jnp.bfloat16

    def out(shape, dtype):
        return jax.ShapeDtypeStruct(shape, dtype)

    reach = 2 * (REACH + CHILDREN)
    size = CHILDREN // per_device
    width = per_device * RANK
    window = 2 * (2 * PLANE + 1)
    links = max(len(out_[link]) for out_ in OUTBOUND for link in LINKS)
    sems = pltpu.SemaphoreType.DMA
    factor, panel, blocks, landed = pl.pallas_call(
        functools.partial(level_kernel, count, parents, targets),
        out_shape=(
            out((per_device, red, red), f32),
            out((per_device, red, RANK), f32),
            out((per_device, targets, RANK, CHILDREN * RANK), f32),
            out((size, per_device, RANK, width), bf16),
        ),
        in_specs=[vmem, vmem, vmem, hbm],
        out_specs=(vmem,) * 4,
        scratch_shapes=[
            pltpu.VMEM((window,) + bases.shape, bf16),
            pltpu.VMEM((window, per_device, red, RANK), bf16),
            pltpu.VMEM((per_device, red, RANK), bf16),
            pltpu.VMEM((per_device, RANK, RANK), f32),
            pltpu.VMEM(bases.shape, bf16),
            pltpu.VMEM((per_device, red, 2 * red + RANK), f32),
            pltpu.VMEM((per_device, red, 2 * red + RANK), f32),
            pltpu.VMEM(near_blocks.shape, bf16),
            pltpu.VMEM((per_device, slots, RANK, 6 * RANK), bf16),
            pltpu.VMEM((per_device, RANK, CHILDREN * RANK), bf16),
            sems((2, len(LINKS), links)),
            sems((2, 2 * PLANE + 1, per_device)),
            sems((2, 2 * PLANE + 1, per_device)),
            sems((2, 2 * PLANE + 1, per_device)),
            sems((2,)),
            sems((per_device,)),
            sems((size,)),
            sems((size,)),
            pltpu.VMEM((per_device, reach, 128), jnp.int32),
            pltpu.SMEM((per_device, reach, 128), jnp.int32),
            sems(()),
        ],
        compiler_params=pltpu.CompilerParams(
            collective_id=0, has_side_effects=True, vmem_limit_bytes=46_500_000
        ),
        name="level",
    )(leaf_nbrs, diag_blocks, bases, near_blocks)

    return pl.pallas_call(
        place_kernel,
        out_shape=(
            out((per_device, red, red), f32),
            out((per_device, red, RANK), f32),
            out((per_device, targets, RANK, CHILDREN * RANK), f32),
            out((width, CHILDREN * RANK), f32),
        ),
        in_specs=[smem, vmem, vmem, vmem, vmem],
        out_specs=(hbm,) * 4,
        scratch_shapes=[
            pltpu.VMEM((width, CHILDREN * RANK), f32),
            sems((targets * per_device + 2 + size,)),
        ],
        compiler_params=pltpu.CompilerParams(vmem_limit_bytes=16_000_000),
        name="place",
    )(parent_nbrs, factor, panel, blocks, landed)


def solution(mesh):
    count = mesh.shape["leaf"]
    in_specs = (
        P("leaf", None, None, None),
        P("leaf", None, None),
        P("leaf", None, None),
        P("leaf", None),
        P(),
    )
    out_specs = (
        P("leaf", None, None),
        P("leaf", None, None),
        P("leaf", None, None, None),
        P("leaf", None),
    )
    return jax.shard_map(
        functools.partial(local, count),
        mesh=mesh,
        in_specs=in_specs,
        out_specs=out_specs,
        check_vma=False,
    )
```

```python
import functools

import jax
import jax.numpy as jnp
from jax import lax
from jax.experimental import pallas as pl
from jax.experimental.pallas import tpu as pltpu
from jax.sharding import PartitionSpec as P

RANK = 128
REACH = 16
CHILDREN = 8
PANEL = 32
PLANE = 4
LINKS = ("x", "y", "up", "down")
MESH = pl.DeviceIdType.MESH
highest = lax.Precision.HIGHEST


def matmul(a, b):
    return jnp.dot(a, b, preferred_element_type=jnp.float32)


def matmul_t(a, b, precision=None):
    return lax.dot_general(
        a, b, (((0,), (0,)), ((), ())), preferred_element_type=jnp.float32, precision=precision
    )


def plan():
    def both(plane, chip):
        return [(plane, chip, 0), (plane, chip, 1)]

    inbound = (
        {
            "x": both(0, 1) + [(0, 3, 0), (-1, 1, 0)],
            "y": both(0, 2) + [(0, 3, 1)] + both(-1, 2),
            "up": both(-1, 0) + [(-1, 1, 1)] + both(-1, 3),
            "down": both(1, 0),
        },
        {
            "x": both(0, 0) + both(0, 2),
            "y": both(0, 3) + both(-1, 3),
            "up": both(-1, 1) + both(-1, 2),
            "down": both(1, 1) + both(1, 0),
        },
        {
            "x": both(0, 3) + both(0, 1),
            "y": both(0, 0) + both(1, 0),
            "up": both(-1, 2) + both(-1, 3),
            "down": both(1, 2) + both(1, 1),
        },
        {
            "x": both(0, 2) + [(0, 0, 0), (1, 2, 0)],
            "y": both(0, 1) + [(0, 0, 1)] + both(1, 1),
            "up": both(-1, 3),
            "down": both(1, 3) + [(1, 2, 1)] + both(1, 0),
        },
    )
    outbound = []
    for place in range(PLANE):
        out = {"x": inbound[place ^ 1]["x"], "y": inbound[place ^ 2]["y"]}
        out["up"] = [(plane + 1, chip, leaf) for plane, chip, leaf in inbound[place]["up"]]
        out["down"] = [(plane - 1, chip, leaf) for plane, chip, leaf in inbound[place]["down"]]
        outbound.append(out)
    held = [{(0, place, leaf): 0 for leaf in range(2)} for place in range(PLANE)]
    arrivals = [[] for _ in range(PLANE)]
    queue = {(place, link): 0 for place in range(PLANE) for link in LINKS}
    now = 0
    while any(queue[place, link] < len(outbound[place][link]) for place, link in queue):
        now += 1
        landed = []
        for (place, link), done in queue.items():
            items = outbound[place][link]
            if done < len(items) and held[place].get(items[done], now) < now:
                target = {"x": place ^ 1, "y": place ^ 2}.get(link, place)
                landed.append((target, inbound[target][link][done]))
                queue[place, link] = done + 1
        for target, item in landed:
            held[target][item] = now
            arrivals[target].append((now, item))
    return outbound, arrivals


OUTBOUND, ARRIVALS = plan()
STEPS = max(now for events in ARRIVALS for now, _ in events)


def shift_of(place, item):
    plane, chip, _ = item
    return PLANE * plane + chip - place


def chunk_order(place):
    ready = {0: 0}
    for now, item in ARRIVALS[place]:
        ready[shift_of(place, item)] = now
    first = [0, (place ^ 1) - place, (place ^ 2) - place, -PLANE, PLANE]
    rest = sorted((now, delta) for delta, now in ready.items() if delta not in first)
    order = first + [delta for _, delta in rest]
    return order, [ready[delta] for delta in order]


def reduce_blocks(diag, bases, bases_t, work, low_corner):
    per_device, leaf_rows = bases.shape[0], bases.shape[1]
    red = leaf_rows - RANK
    row_id = lax.broadcasted_iota(jnp.int32, (red, red), 0)
    col_id = lax.broadcasted_iota(jnp.int32, (red, red), 1)
    for leaf in range(per_device):
        basis = bases[leaf]
        basis_t = basis.T
        bases_t[leaf] = basis_t
        half = matmul(basis_t, diag[leaf]).astype(jnp.bfloat16)
        dense = matmul(half, basis)
        top = dense[:red, :red]
        work[leaf, :, :red] = 0.5 * (top + top.T)
        work[leaf, :, red : red + RANK] = dense[:red, red:]
        work[leaf, :, red + RANK :] = (row_id == col_id).astype(jnp.float32)
        low_corner[leaf] = dense[red:, red:]


def eliminate(shift, turned, work, rows, serve):
    per_device, red = work.shape[0], work.shape[1]
    wide = 2 * red + RANK
    row_id = lax.broadcasted_iota(jnp.int32, (red, red), 0)
    col_id = lax.broadcasted_iota(jnp.int32, (red, red), 1)
    sub = lax.broadcasted_iota(jnp.int32, (PANEL, 1), 0)
    for start in range(0, red, PANEL):
        strips = [work[leaf, start : start + PANEL, :] for leaf in range(per_device)]
        for k in range(PANEL):
            for leaf in range(per_device):
                strip = strips[leaf]
                column = strip[:, start + k : start + k + 1]
                ratio = jnp.where(sub > k, column / column[k : k + 1], 0.0)
                strips[leaf] = strip - ratio * strip[k : k + 1, :]
        lane = lax.broadcasted_iota(jnp.int32, (PANEL, wide), 1)
        line = lax.broadcasted_iota(jnp.int32, (PANEL, wide), 0)
        for leaf in range(per_device):
            strip = strips[leaf]
            pivots = jnp.sum(jnp.where(lane == line + start, strip, 0.0), axis=1, keepdims=True)
            strip = strip * (1.0 / jnp.sqrt(pivots))
            rows[leaf, start : start + PANEL, :] = strip
            if start + PANEL < red:
                work[leaf] = work[leaf] - matmul_t(strip[:, :red], strip, highest)
        serve(start // PANEL)
    for leaf in range(per_device):
        solved = rows[leaf, :, red : red + RANK]
        inverse = jnp.where(col_id <= row_id, rows[leaf, :, red + RANK :], 0.0)
        moved = matmul_t(inverse, solved, highest)
        shift[leaf] = moved.astype(jnp.bfloat16)
        back = -moved.astype(jnp.bfloat16).astype(jnp.float32).T
        turned[leaf, :, :red] = back.astype(jnp.bfloat16)
        turned[leaf, :, red:] = back.astype(jnp.bfloat16)


def finish_factor(factor, panel, skeleton, rows, low_corner):
    per_device, red = rows.shape[0], rows.shape[1]
    row_id = lax.broadcasted_iota(jnp.int32, (red, red), 0)
    col_id = lax.broadcasted_iota(jnp.int32, (red, red), 1)
    for leaf in range(per_device):
        solved = rows[leaf, :, red : red + RANK]
        panel[leaf] = solved
        skeleton[leaf] = low_corner[leaf] - matmul_t(solved, solved, highest)
        upper = jnp.where(col_id >= row_id, rows[leaf, :, :red], 0.0)
        factor[leaf] = upper.T


def split(values):
    high = values.astype(jnp.bfloat16)
    return high, (values - high.astype(jnp.float32)).astype(jnp.bfloat16)


def level_kernel(
    count,
    parents,
    targets,
    nbrs,
    diag,
    bases,
    near,
    factor,
    panel,
    blocks,
    landed,
    win_bases,
    win_shift,
    diag_in,
    nbrs_in,
    low_corner,
    skeleton,
    turned,
    bases_t,
    work,
    rows,
    near_in,
    halves,
    lefts,
    diagonal,
    send,
    recv,
    pass_send,
    pass_recv,
    in_sem,
    near_sem,
    row_send,
    row_recv,
    found,
    lookup,
    found_sem,
):
    per_device, slots = near_in.shape[0], near_in.shape[1]
    red = rows.shape[1]
    total = count // 2
    me = lax.axis_index("leaf")
    core, chip = me % 2, me // 2
    sibling = me + 1 - 2 * core
    place = chip % PLANE
    size = CHILDREN // per_device
    seat = me % size
    across = me + 2 * (1 - 2 * (place % 2))
    along = me + 4 * (1 - 2 * (place // 2))
    device = {"x": across, "y": along, "up": me + 2 * PLANE, "down": me - 2 * PLANE}
    present = {"up": chip + PLANE < total, "down": chip - PLANE >= 0}
    far = across + 1 - 2 * core

    fetches = [
        pltpu.make_async_copy(near.at[leaf], near_in.at[leaf], near_sem.at[leaf])
        for leaf in range(per_device)
    ]
    here = 2 * PLANE + core
    inputs = [
        pltpu.make_async_copy(source, target, in_sem.at[n])
        for n, (source, target) in enumerate(
            ((nbrs, nbrs_in), (bases, win_bases.at[here]), (diag, diag_in))
        )
    ]
    for copy in inputs + fetches:
        copy.start()

    barrier = pltpu.get_barrier_semaphore()
    for other in (sibling, across, along, far):
        pl.semaphore_signal(barrier, inc=1, device_id=(other,), device_id_type=MESH)
    peers = jnp.int32(4)
    for link in ("up", "down"):

        @pl.when(present[link])
        def _(link=link):
            pl.semaphore_signal(barrier, inc=1, device_id=(device[link],), device_id_type=MESH)

        peers = peers + present[link].astype(jnp.int32)

    windows = (win_bases, win_shift)

    def exists(delta):
        return (chip + delta >= 0) & (chip + delta < total)

    def slot_of(delta, holder):
        return 2 * (PLANE + delta) + holder

    def hop(kind, at, link, order):
        item = OUTBOUND[at][link][order]
        delta = shift_of(at, item)
        moved = {"x": at - (at ^ 1), "y": at - (at ^ 2), "up": -PLANE, "down": PLANE}[link]
        window = windows[kind]
        leaf = item[2]
        return pltpu.make_async_remote_copy(
            src_ref=window.at[slot_of(delta, core), leaf],
            dst_ref=window.at[slot_of(delta + moved, core), leaf],
            send_sem=send.at[kind, LINKS.index(link), order],
            recv_sem=recv.at[kind, PLANE + delta + moved, leaf],
            device_id=(device[link],),
            device_id_type=MESH,
        )

    def arrival(kind, delta, leaf):
        window = windows[kind]
        there = window.at[slot_of(delta, core), leaf]
        return pltpu.make_async_remote_copy(
            src_ref=there,
            dst_ref=there,
            send_sem=send.at[kind, 0, 0],
            recv_sem=recv.at[kind, PLANE + delta, leaf],
            device_id=(sibling,),
            device_id_type=MESH,
        )

    def relay(kind, delta, leaf):
        window = windows[kind]
        there = window.at[slot_of(delta, core), leaf]
        return pltpu.make_async_remote_copy(
            src_ref=there,
            dst_ref=there,
            send_sem=pass_send.at[kind, PLANE + delta, leaf],
            recv_sem=pass_recv.at[kind, PLANE + delta, leaf],
            device_id=(sibling,),
            device_id_type=MESH,
        )

    def relayed(kind, delta, leaf):
        window = windows[kind]
        there = window.at[slot_of(delta, 1 - core), leaf]
        return pltpu.make_async_remote_copy(
            src_ref=there,
            dst_ref=there,
            send_sem=pass_send.at[kind, PLANE + delta, leaf],
            recv_sem=pass_recv.at[kind, PLANE + delta, leaf],
            device_id=(sibling,),
            device_id_type=MESH,
        )

    def on_links(kind, at, item, act):
        for link in LINKS:
            for order, entry in enumerate(OUTBOUND[at][link]):
                if entry == item:
                    if link in present:
                        pl.when(present[link])(lambda: act(hop(kind, at, link, order)))
                    else:
                        act(hop(kind, at, link, order))

    def start(copy):
        copy.start()

    def stop(copy):
        copy.wait_send()

    def by_place(act):
        for at in range(PLANE):
            pl.when(place == at)(lambda: act(at))

    def dispatch(kind):
        def act(at):
            for leaf in range(per_device):
                on_links(kind, at, (0, at, leaf), start)

        by_place(act)
        for leaf in range(per_device):
            relay(kind, 0, leaf).start()

    def serve(kind, step):
        def act(at):
            for now, item in ARRIVALS[at]:
                if now == step:
                    delta, leaf = shift_of(at, item), item[2]

                    def one():
                        arrival(kind, delta, leaf).wait_recv()
                        on_links(kind, at, item, start)
                        relay(kind, delta, leaf).start()

                    if item[0] == 0:
                        one()
                    else:
                        pl.when(exists(delta))(one)

        by_place(act)

    def finish(kind):
        def act(at):
            for leaf in range(per_device):
                on_links(kind, at, (0, at, leaf), stop)
            for _, item in ARRIVALS[at]:
                delta, leaf = shift_of(at, item), item[2]

                def one():
                    on_links(kind, at, item, stop)
                    relay(kind, delta, leaf).wait_send()

                if item[0] == 0:
                    one()
                else:
                    pl.when(exists(delta))(one)

        by_place(act)
        for leaf in range(per_device):
            relay(kind, 0, leaf).wait_send()

    number = me * per_device
    parent = number // CHILDREN
    low = jnp.clip(parent - targets // 2, 0, parents - targets)
    home = parent - low
    blocks[...] = jnp.zeros_like(blocks)
    halves[:, slots] = jnp.zeros_like(halves[:, slots])
    reach = found.shape[1]
    offset = lax.broadcasted_iota(jnp.int32, (reach, slots), 0) - reach // 2
    order = lax.broadcasted_iota(jnp.int32, (reach, slots), 1)
    inputs[0].wait()
    for leaf in range(per_device):
        away = offset + number + leaf
        hit = (nbrs_in[leaf : leaf + 1, :] == away) & (away >= 0)
        slot = jnp.max(jnp.where(hit, order, -1), axis=1, keepdims=True)
        found[leaf] = jnp.broadcast_to(jnp.where(slot < 0, slots, slot), found.shape[1:])
    table = pltpu.make_async_copy(found, lookup, found_sem)
    table.start()
    for copy in inputs[1:]:
        copy.wait()
    reduce_blocks(diag_in, win_bases.at[here], bases_t, work, low_corner)
    pl.semaphore_wait(barrier, peers)
    dispatch(0)

    def between(panel_done):
        if panel_done > 0 and panel_done < red // PANEL - 1:
            serve(0, panel_done)

    eliminate(win_shift.at[here], turned, work, rows, between)
    dispatch(1)

    unroll = max(n for n in range(1, 14) if slots % n == 0)

    def project(turn):
        for k in range(unroll):
            n = turn * unroll + k
            for leaf in range(per_device):
                halves[leaf, n] = matmul(bases_t[leaf], near_in[leaf, n]).astype(jnp.bfloat16)

    orders = [chunk_order(at) for at in range(PLANE)]
    chunks = len(orders[0][0])

    def pick(values):
        chosen = jnp.int32(values[0])
        for at in range(1, PLANE):
            chosen = jnp.where(place == at, jnp.int32(values[at]), chosen)
        return chosen

    deltas = [pick([order[0][turn] for order in orders]) for turn in range(chunks)]
    steps = [max(order[1][turn] for order in orders) for turn in range(chunks)]

    def pairs_of(turn):
        delta = deltas[turn]
        for holder in range(2):
            for leaf in range(per_device):
                other = ((chip + delta) * 2 + holder) * per_device + leaf
                column = pl.multiple_of((other % CHILDREN) * RANK, RANK)
                yield holder, leaf, slot_of(delta, holder), other, other // CHILDREN - low, column

    def keep(turn, values):
        for (other, row, column, mine), act in values:
            if turn in (3, 4):
                apart = other - number - mine
                pl.when((apart <= REACH) & (apart >= -REACH))(lambda: act(row, column, mine))
            else:
                act(row, column, mine)

    def first_half(turn):
        for leaf in range(per_device):
            relayed(0, deltas[turn], leaf).wait_recv()
        coupled = {}
        targets_of = {}
        for holder, leaf, slot, other, row, column in pairs_of(turn):
            left = []
            for mine in range(per_device):
                n = lookup[mine, other - number - mine + reach // 2, 0]
                left.append(halves[mine, n])
                targets_of[holder, leaf, mine] = (other, row, column, mine)
            both = matmul(jnp.concatenate(left, axis=0), win_bases[slot, leaf])
            for mine in range(per_device):
                part = both[mine * 2 * RANK : (mine + 1) * 2 * RANK]
                high, low_part = split(part[red:, :red])
                here_rows = pl.ds(mine * RANK, RANK)
                lefts[turn, holder, leaf, here_rows, :red] = high
                lefts[turn, holder, leaf, here_rows, red:] = low_part
                coupled[holder, leaf, mine] = (split(part[:red, red:]), part[red:, red:])
        kept = []
        for holder in range(2):
            for mine in range(per_device):
                tall = [
                    jnp.concatenate(coupled[holder, leaf, mine][0], axis=0)
                    for leaf in range(per_device)
                ]
                moved = matmul(turned[mine], jnp.concatenate(tall, axis=1))
                for leaf in range(per_device):
                    value = coupled[holder, leaf, mine][1] + moved[:, leaf * RANK : (leaf + 1) * RANK]

                    def act(row, column, mine, value=value):
                        blocks[mine, row, :, pl.ds(column, RANK)] = value

                    kept.append((targets_of[holder, leaf, mine], act))
        keep(turn, kept)

    def second_half(turn):
        for leaf in range(per_device):
            relayed(1, deltas[turn], leaf).wait_recv()
        kept = []
        for holder, leaf, slot, other, row, column in pairs_of(turn):
            moved = win_shift[slot, leaf]
            both = matmul(lefts[turn, holder, leaf], jnp.concatenate([moved, moved], axis=0))
            for mine in range(per_device):
                value = both[mine * RANK : (mine + 1) * RANK]

                def act(row, column, mine, value=value):
                    spot = blocks[mine, row, :, pl.ds(column, RANK)]
                    blocks[mine, row, :, pl.ds(column, RANK)] = spot - value

                kept.append(((other, row, column, mine), act))
        keep(turn, kept)

    def run(half, turn):
        pl.when(exists(deltas[turn]))(lambda: half(turn))

    def row_copy(t):
        other = (seat + t) % size
        width = per_device * RANK
        return pltpu.make_async_remote_copy(
            src_ref=diagonal.at[:, :, pl.ds(pl.multiple_of(other * width, 128), width)],
            dst_ref=landed.at[size - t],
            send_sem=row_send.at[t],
            recv_sem=row_recv.at[size - t],
            device_id=(me - seat + other,),
            device_id_type=MESH,
        )

    served = [red // PANEL - 2, 0]

    def serve_to(kind, step):
        while served[kind] < step:
            served[kind] += 1
            serve(kind, served[kind])

    for copy in fetches:
        copy.wait()
    table.wait()
    for turn in range(slots // unroll):
        project(turn)
        serve_to(0, red // PANEL - 1 + turn)
    finish_factor(factor, panel, skeleton, rows, low_corner)
    near_chunks = [turn for turn in range(chunks) if steps[turn] <= 2]
    far_chunks = [turn for turn in range(chunks) if steps[turn] > 2]
    for turn in near_chunks[:2]:
        run(first_half, turn)
    serve_to(1, 2)
    for turn in near_chunks[:2]:
        run(second_half, turn)
    for leaf in range(per_device):
        column = pl.multiple_of(((number + leaf) % CHILDREN) * RANK, RANK)
        blocks[leaf, home, :, pl.ds(column, RANK)] = skeleton[leaf]
    for leaf in range(per_device):
        diagonal[leaf] = blocks[leaf, home].astype(jnp.bfloat16)
    for t in range(1, size):
        row_copy(t).start()
    for turn in near_chunks[2:]:
        run(first_half, turn)
    serve_to(0, STEPS)
    for turn in near_chunks[2:]:
        run(second_half, turn)
    serve_to(1, 3)
    for turn in far_chunks:
        run(first_half, turn)
    for turn in far_chunks:
        serve_to(1, steps[turn])
        run(second_half, turn)
    serve_to(1, STEPS)

    finish(0)
    finish(1)
    for t in range(1, size):
        row_copy(size - t).wait_recv()
    for t in range(1, size):
        row_copy(t).wait_send()


def place_kernel(
    parents, factor, panel, blocks, landed, factor_out, panel_out, merged, block_out, block, sems
):
    per_device, targets = blocks.shape[0], blocks.shape[1]
    size = landed.shape[0]
    width = per_device * RANK
    me = lax.axis_index("leaf")
    seat = me % size
    parent = me * per_device // CHILDREN
    low = jnp.clip(parent - targets // 2, 0, parents.shape[0] - targets)
    copies = []

    def put(source, target):
        copy = pltpu.make_async_copy(source, target, sems.at[len(copies)])
        copy.start()
        copies.append(copy)

    for q in range(targets):
        row = parents[parent, q] - low
        for leaf in range(per_device):
            put(blocks.at[leaf, row], merged.at[leaf, q])
    put(factor, factor_out)
    put(panel, panel_out)
    for t in range(size):
        columns = pl.ds(pl.multiple_of(((seat + t) % size) * width, 128), width)
        mine = blocks[:, parent - low, :, columns].reshape(width, width)
        if t == 0:
            theirs = mine
        else:
            theirs = landed[t].reshape(width, width).astype(jnp.float32)
        block[:, columns] = 0.5 * (mine + theirs.T)
        put(block.at[:, columns], block_out.at[:, columns])
    for copy in copies:
        copy.wait()


def local(count, near_blocks, diag_blocks, bases, leaf_nbrs, parent_nbrs):
    per_device, leaf_rows = bases.shape[0], bases.shape[1]
    red = leaf_rows - RANK
    slots = near_blocks.shape[1]
    parents, targets = parent_nbrs.shape
    assert per_device == 2 and REACH == 4 * PLANE
    vmem = pl.BlockSpec(memory_space=pltpu.VMEM)
    smem = pl.BlockSpec(memory_space=pltpu.SMEM)
    hbm = pl.BlockSpec(memory_space=pltpu.HBM)
    f32, bf16 = jnp.float32, jnp.bfloat16

    def out(shape, dtype):
        return jax.ShapeDtypeStruct(shape, dtype)

    reach = 2 * (REACH + CHILDREN)
    size = CHILDREN // per_device
    width = per_device * RANK
    window = 2 * (2 * PLANE + 1)
    links = max(len(out_[link]) for out_ in OUTBOUND for link in LINKS)
    sems = pltpu.SemaphoreType.DMA
    factor, panel, blocks, landed = pl.pallas_call(
        functools.partial(level_kernel, count, parents, targets),
        out_shape=(
            out((per_device, red, red), f32),
            out((per_device, red, RANK), f32),
            out((per_device, targets, RANK, CHILDREN * RANK), f32),
            out((size, per_device, RANK, width), bf16),
        ),
        in_specs=[hbm] * 4,
        out_specs=(vmem,) * 4,
        scratch_shapes=[
            pltpu.VMEM((window,) + bases.shape, bf16),
            pltpu.VMEM((window, per_device, red, RANK), bf16),
            pltpu.VMEM(diag_blocks.shape, bf16),
            pltpu.VMEM(leaf_nbrs.shape, jnp.int32),
            pltpu.VMEM((per_device, RANK, RANK), f32),
            pltpu.VMEM((per_device, RANK, RANK), f32),
            pltpu.VMEM((per_device, RANK, 2 * red), bf16),
            pltpu.VMEM(bases.shape, bf16),
            pltpu.VMEM((per_device, red, 2 * red + RANK), f32),
            pltpu.VMEM((per_device, red, 2 * red + RANK), f32),
            pltpu.VMEM(near_blocks.shape, bf16),
            pltpu.VMEM((per_device, slots + 1) + near_blocks.shape[2:], bf16),
            pltpu.VMEM((2 * PLANE + 1, 2, per_device, per_device * RANK, 2 * red), bf16),
            pltpu.VMEM((per_device, RANK, CHILDREN * RANK), bf16),
            sems((2, len(LINKS), links)),
            sems((2, 2 * PLANE + 1, per_device)),
            sems((2, 2 * PLANE + 1, per_device)),
            sems((2, 2 * PLANE + 1, per_device)),
            sems((3,)),
            sems((per_device,)),
            sems((size,)),
            sems((size,)),
            pltpu.VMEM((per_device, reach, 128), jnp.int32),
            pltpu.SMEM((per_device, reach, 128), jnp.int32),
            sems(()),
        ],
        compiler_params=pltpu.CompilerParams(
            collective_id=0, has_side_effects=True, vmem_limit_bytes=46_500_000
        ),
        name="level",
    )(leaf_nbrs, diag_blocks, bases, near_blocks)

    return pl.pallas_call(
        place_kernel,
        out_shape=(
            out((per_device, red, red), f32),
            out((per_device, red, RANK), f32),
            out((per_device, targets, RANK, CHILDREN * RANK), f32),
            out((width, CHILDREN * RANK), f32),
        ),
        in_specs=[smem, vmem, vmem, vmem, vmem],
        out_specs=(hbm,) * 4,
        scratch_shapes=[
            pltpu.VMEM((width, CHILDREN * RANK), f32),
            sems((targets * per_device + 2 + size,)),
        ],
        compiler_params=pltpu.CompilerParams(vmem_limit_bytes=16_000_000),
        name="place",
    )(parent_nbrs, factor, panel, blocks, landed)


def solution(mesh):
    count = mesh.shape["leaf"]
    in_specs = (
        P("leaf", None, None, None),
        P("leaf", None, None),
        P("leaf", None, None),
        P("leaf", None),
        P(),
    )
    out_specs = (
        P("leaf", None, None),
        P("leaf", None, None),
        P("leaf", None, None, None),
        P("leaf", None),
    )
    return jax.shard_map(
        functools.partial(local, count),
        mesh=mesh,
        in_specs=in_specs,
        out_specs=out_specs,
        check_vma=False,
    )
```

```python
import functools

import jax
import jax.numpy as jnp
from jax import lax
from jax.experimental import pallas as pl
from jax.experimental.pallas import tpu as pltpu
from jax.sharding import PartitionSpec as P

RANK = 128
REACH = 16
CHILDREN = 8
PANEL = 32
PLANE = 4
LINKS = ("x", "y", "up", "down")
MESH = pl.DeviceIdType.MESH
highest = lax.Precision.HIGHEST


def matmul(a, b):
    return jnp.dot(a, b, preferred_element_type=jnp.float32)


def matmul_t(a, b, precision=None):
    return lax.dot_general(
        a, b, (((0,), (0,)), ((), ())), preferred_element_type=jnp.float32, precision=precision
    )


def halves_of(plane, chip):
    return [(plane, chip, 0), (plane, chip, 1)]


def whole(plane, chip):
    return [(plane, chip, None)]


BASES_IN = (
    {
        "x": halves_of(0, 1) + [(0, 3, 0), (-1, 1, 0)],
        "y": halves_of(0, 2) + [(0, 3, 1)] + halves_of(-1, 2),
        "up": halves_of(-1, 0) + [(-1, 1, 1)] + halves_of(-1, 3),
        "down": halves_of(1, 0),
    },
    {
        "x": halves_of(0, 0) + halves_of(0, 2),
        "y": halves_of(0, 3) + halves_of(-1, 3),
        "up": halves_of(-1, 1) + halves_of(-1, 2),
        "down": halves_of(1, 1) + halves_of(1, 0),
    },
    {
        "x": halves_of(0, 3) + halves_of(0, 1),
        "y": halves_of(0, 0) + halves_of(1, 0),
        "up": halves_of(-1, 2) + halves_of(-1, 3),
        "down": halves_of(1, 2) + halves_of(1, 1),
    },
    {
        "x": halves_of(0, 2) + [(0, 0, 0), (1, 2, 0)],
        "y": halves_of(0, 1) + [(0, 0, 1)] + halves_of(1, 1),
        "up": halves_of(-1, 3),
        "down": halves_of(1, 3) + [(1, 2, 1)] + halves_of(1, 0),
    },
)
SHIFTS_IN = (
    {
        "x": whole(0, 1) + whole(-1, 1),
        "y": whole(0, 2) + whole(0, 3) + whole(-1, 2),
        "up": whole(-1, 0) + whole(-1, 3),
        "down": whole(1, 0),
    },
    {
        "x": whole(0, 0) + whole(0, 2),
        "y": whole(0, 3) + whole(-1, 3),
        "up": whole(-1, 1) + whole(-1, 2),
        "down": whole(1, 1) + whole(1, 0),
    },
    {
        "x": whole(0, 3) + whole(0, 1),
        "y": whole(0, 0) + whole(1, 0),
        "up": whole(-1, 2) + whole(-1, 3),
        "down": whole(1, 2) + whole(1, 1),
    },
    {
        "x": whole(0, 2) + whole(1, 2),
        "y": whole(0, 1) + whole(0, 0) + whole(1, 1),
        "up": whole(-1, 3),
        "down": whole(1, 3) + whole(1, 0),
    },
)


def plan(inbound):
    outbound = []
    for place in range(PLANE):
        out = {"x": inbound[place ^ 1]["x"], "y": inbound[place ^ 2]["y"]}
        out["up"] = [(plane + 1, chip, leaf) for plane, chip, leaf in inbound[place]["up"]]
        out["down"] = [(plane - 1, chip, leaf) for plane, chip, leaf in inbound[place]["down"]]
        outbound.append(out)
    held = [{(0, place, leaf): 0 for leaf in (0, 1, None)} for place in range(PLANE)]
    arrivals = [[] for _ in range(PLANE)]
    queue = {(place, link): 0 for place in range(PLANE) for link in LINKS}
    now = 0
    while any(queue[place, link] < len(outbound[place][link]) for place, link in queue):
        now += 1
        landed = []
        for (place, link), done in queue.items():
            items = outbound[place][link]
            if done < len(items) and held[place].get(items[done], now) < now:
                target = {"x": place ^ 1, "y": place ^ 2}.get(link, place)
                landed.append((target, inbound[target][link][done]))
                queue[place, link] = done + 1
        for target, item in landed:
            held[target][item] = now
            arrivals[target].append((now, item))
    return outbound, arrivals, now


OUTBOUND, ARRIVALS, STEPS = zip(plan(BASES_IN), plan(SHIFTS_IN))


def shift_of(place, item):
    plane, chip, _ = item
    return PLANE * plane + chip - place


def chunk_order(place):
    ready = [{0: 0}, {0: 0}]
    for kind in range(2):
        for now, item in ARRIVALS[kind][place]:
            ready[kind][shift_of(place, item)] = now
    first = [0, (place ^ 1) - place, (place ^ 2) - place, -PLANE, PLANE]
    rest = sorted((ready[1][delta], now, delta) for delta, now in ready[0].items() if delta not in first)
    order = first + [delta for _, _, delta in rest]
    return order, [(ready[0][delta], ready[1][delta]) for delta in order]


def reduce_blocks(diag, bases, bases_t, work, low_corner):
    per_device, leaf_rows = bases.shape[0], bases.shape[1]
    red = leaf_rows - RANK
    row_id = lax.broadcasted_iota(jnp.int32, (red, red), 0)
    col_id = lax.broadcasted_iota(jnp.int32, (red, red), 1)
    for leaf in range(per_device):
        basis = bases[leaf]
        basis_t = basis.T
        bases_t[leaf] = basis_t
        half = matmul(basis_t, diag[leaf]).astype(jnp.bfloat16)
        dense = matmul(half, basis)
        top = dense[:red, :red]
        work[leaf, :, :red] = 0.5 * (top + top.T)
        work[leaf, :, red : red + RANK] = dense[:red, red:]
        work[leaf, :, red + RANK :] = (row_id == col_id).astype(jnp.float32)
        low_corner[leaf] = dense[red:, red:]


def eliminate(shift, turned, work, rows, serve):
    per_device, red = work.shape[0], work.shape[1]
    wide = 2 * red + RANK
    row_id = lax.broadcasted_iota(jnp.int32, (red, red), 0)
    col_id = lax.broadcasted_iota(jnp.int32, (red, red), 1)
    sub = lax.broadcasted_iota(jnp.int32, (PANEL, 1), 0)
    for start in range(0, red, PANEL):
        strips = [work[leaf, start : start + PANEL, :] for leaf in range(per_device)]
        for k in range(PANEL):
            for leaf in range(per_device):
                strip = strips[leaf]
                column = strip[:, start + k : start + k + 1]
                ratio = jnp.where(sub > k, column / column[k : k + 1], 0.0)
                strips[leaf] = strip - ratio * strip[k : k + 1, :]
        lane = lax.broadcasted_iota(jnp.int32, (PANEL, wide), 1)
        line = lax.broadcasted_iota(jnp.int32, (PANEL, wide), 0)
        for leaf in range(per_device):
            strip = strips[leaf]
            pivots = jnp.sum(jnp.where(lane == line + start, strip, 0.0), axis=1, keepdims=True)
            strip = strip * (1.0 / jnp.sqrt(pivots))
            rows[leaf, start : start + PANEL, :] = strip
            if start + PANEL < red:
                work[leaf] = work[leaf] - matmul_t(strip[:, :red], strip, highest)
        serve(start // PANEL)
    for leaf in range(per_device):
        solved = rows[leaf, :, red : red + RANK]
        inverse = jnp.where(col_id <= row_id, rows[leaf, :, red + RANK :], 0.0)
        moved = matmul_t(inverse, solved, highest)
        shift[leaf] = moved.astype(jnp.bfloat16)
        back = -moved.astype(jnp.bfloat16).astype(jnp.float32).T
        turned[leaf, :, :red] = back.astype(jnp.bfloat16)
        turned[leaf, :, red:] = back.astype(jnp.bfloat16)


def finish_factor(factor, panel, skeleton, rows, low_corner):
    per_device, red = rows.shape[0], rows.shape[1]
    row_id = lax.broadcasted_iota(jnp.int32, (red, red), 0)
    col_id = lax.broadcasted_iota(jnp.int32, (red, red), 1)
    for leaf in range(per_device):
        solved = rows[leaf, :, red : red + RANK]
        panel[leaf] = solved
        skeleton[leaf] = low_corner[leaf] - matmul_t(solved, solved, highest)
        upper = jnp.where(col_id >= row_id, rows[leaf, :, :red], 0.0)
        factor[leaf] = upper.T


def split(values):
    high = values.astype(jnp.bfloat16)
    return high, (values - high.astype(jnp.float32)).astype(jnp.bfloat16)


def level_kernel(
    count,
    parents,
    targets,
    nbrs,
    diag,
    bases,
    near,
    factor,
    panel,
    blocks,
    landed,
    win_bases,
    win_shift,
    diag_in,
    nbrs_in,
    low_corner,
    skeleton,
    turned,
    bases_t,
    work,
    rows,
    near_in,
    halves,
    lefts,
    diagonal,
    send,
    recv,
    pass_send,
    pass_recv,
    in_sem,
    near_sem,
    row_send,
    row_recv,
    found,
    lookup,
    found_sem,
):
    per_device, slots = near_in.shape[0], near_in.shape[1]
    red = rows.shape[1]
    total = count // 2
    me = lax.axis_index("leaf")
    core, chip = me % 2, me // 2
    sibling = me + 1 - 2 * core
    place = chip % PLANE
    size = CHILDREN // per_device
    seat = me % size
    across = me + 2 * (1 - 2 * (place % 2))
    along = me + 4 * (1 - 2 * (place // 2))
    device = {"x": across, "y": along, "up": me + 2 * PLANE, "down": me - 2 * PLANE}
    present = {"up": chip + PLANE < total, "down": chip - PLANE >= 0}
    far = across + 1 - 2 * core

    fetches = [
        pltpu.make_async_copy(near.at[leaf], near_in.at[leaf], near_sem.at[leaf])
        for leaf in range(per_device)
    ]
    here = 2 * PLANE + core
    inputs = [
        pltpu.make_async_copy(source, target, in_sem.at[n])
        for n, (source, target) in enumerate(
            ((nbrs, nbrs_in), (bases, win_bases.at[here]), (diag, diag_in))
        )
    ]
    for copy in inputs + fetches:
        copy.start()

    barrier = pltpu.get_barrier_semaphore()
    for other in (sibling, across, along, far):
        pl.semaphore_signal(barrier, inc=1, device_id=(other,), device_id_type=MESH)
    peers = jnp.int32(4)
    for link in ("up", "down"):

        @pl.when(present[link])
        def _(link=link):
            pl.semaphore_signal(barrier, inc=1, device_id=(device[link],), device_id_type=MESH)

        peers = peers + present[link].astype(jnp.int32)

    windows = (win_bases, win_shift)

    def exists(delta):
        return (chip + delta >= 0) & (chip + delta < total)

    def slot_of(delta, holder):
        return 2 * (PLANE + delta) + holder

    def block_of(kind, delta, holder, leaf):
        block = windows[kind].at[slot_of(delta, holder)]
        return block if leaf is None else block.at[leaf]

    def hop(kind, at, link, order):
        item = OUTBOUND[kind][at][link][order]
        delta, leaf = shift_of(at, item), item[2]
        moved = {"x": at - (at ^ 1), "y": at - (at ^ 2), "up": -PLANE, "down": PLANE}[link]
        return pltpu.make_async_remote_copy(
            src_ref=block_of(kind, delta, core, leaf),
            dst_ref=block_of(kind, delta + moved, core, leaf),
            send_sem=send.at[kind, LINKS.index(link), order],
            recv_sem=recv.at[kind, PLANE + delta + moved, leaf or 0],
            device_id=(device[link],),
            device_id_type=MESH,
        )

    def arrival(kind, delta, leaf):
        there = block_of(kind, delta, core, leaf)
        return pltpu.make_async_remote_copy(
            src_ref=there,
            dst_ref=there,
            send_sem=send.at[kind, 0, 0],
            recv_sem=recv.at[kind, PLANE + delta, leaf or 0],
            device_id=(sibling,),
            device_id_type=MESH,
        )

    def relay(kind, delta, leaf):
        there = block_of(kind, delta, core, leaf)
        return pltpu.make_async_remote_copy(
            src_ref=there,
            dst_ref=there,
            send_sem=pass_send.at[kind, PLANE + delta, leaf or 0],
            recv_sem=pass_recv.at[kind, PLANE + delta, leaf or 0],
            device_id=(sibling,),
            device_id_type=MESH,
        )

    def relayed(kind, delta, leaf):
        there = block_of(kind, delta, 1 - core, leaf)
        return pltpu.make_async_remote_copy(
            src_ref=there,
            dst_ref=there,
            send_sem=pass_send.at[kind, PLANE + delta, leaf or 0],
            recv_sem=pass_recv.at[kind, PLANE + delta, leaf or 0],
            device_id=(sibling,),
            device_id_type=MESH,
        )

    def parts(kind):
        return (None,) if kind else range(per_device)

    def on_links(kind, at, item, act):
        for link in LINKS:
            for order, entry in enumerate(OUTBOUND[kind][at][link]):
                if entry == item:
                    if link in present:
                        pl.when(present[link])(lambda: act(hop(kind, at, link, order)))
                    else:
                        act(hop(kind, at, link, order))

    def start(copy):
        copy.start()

    def stop(copy):
        copy.wait_send()

    def by_place(act):
        for at in range(PLANE):
            pl.when(place == at)(lambda: act(at))

    def dispatch(kind):
        def act(at):
            for leaf in parts(kind):
                on_links(kind, at, (0, at, leaf), start)

        by_place(act)
        for leaf in parts(kind):
            relay(kind, 0, leaf).start()

    def serve(kind, step):
        def act(at):
            for now, item in ARRIVALS[kind][at]:
                if now == step:
                    delta, leaf = shift_of(at, item), item[2]

                    def one():
                        arrival(kind, delta, leaf).wait_recv()
                        on_links(kind, at, item, start)
                        relay(kind, delta, leaf).start()

                    if item[0] == 0:
                        one()
                    else:
                        pl.when(exists(delta))(one)

        by_place(act)

    def finish(kind):
        def act(at):
            for leaf in parts(kind):
                on_links(kind, at, (0, at, leaf), stop)
            for _, item in ARRIVALS[kind][at]:
                delta, leaf = shift_of(at, item), item[2]

                def one():
                    on_links(kind, at, item, stop)
                    relay(kind, delta, leaf).wait_send()

                if item[0] == 0:
                    one()
                else:
                    pl.when(exists(delta))(one)

        by_place(act)
        for leaf in parts(kind):
            relay(kind, 0, leaf).wait_send()

    number = me * per_device
    parent = number // CHILDREN
    low = jnp.clip(parent - targets // 2, 0, parents - targets)
    home = parent - low
    blocks[...] = jnp.zeros_like(blocks)
    halves[:, slots] = jnp.zeros_like(halves[:, slots])
    reach = found.shape[1]
    offset = lax.broadcasted_iota(jnp.int32, (reach, slots), 0) - reach // 2
    order = lax.broadcasted_iota(jnp.int32, (reach, slots), 1)
    inputs[0].wait()
    for leaf in range(per_device):
        away = offset + number + leaf
        hit = (nbrs_in[leaf : leaf + 1, :] == away) & (away >= 0)
        slot = jnp.max(jnp.where(hit, order, -1), axis=1, keepdims=True)
        found[leaf] = jnp.broadcast_to(jnp.where(slot < 0, slots, slot), found.shape[1:])
    table = pltpu.make_async_copy(found, lookup, found_sem)
    table.start()
    for copy in inputs[1:]:
        copy.wait()
    reduce_blocks(diag_in, win_bases.at[here], bases_t, work, low_corner)
    pl.semaphore_wait(barrier, peers)
    dispatch(0)

    def between(panel_done):
        if panel_done > 0 and panel_done < red // PANEL - 1:
            serve(0, panel_done)

    eliminate(win_shift.at[here], turned, work, rows, between)
    dispatch(1)

    unroll = max(n for n in range(1, 14) if slots % n == 0)

    def project(turn):
        for k in range(unroll):
            n = turn * unroll + k
            for leaf in range(per_device):
                halves[leaf, n] = matmul(bases_t[leaf], near_in[leaf, n]).astype(jnp.bfloat16)

    orders = [chunk_order(at) for at in range(PLANE)]
    chunks = len(orders[0][0])

    def pick(values):
        chosen = jnp.int32(values[0])
        for at in range(1, PLANE):
            chosen = jnp.where(place == at, jnp.int32(values[at]), chosen)
        return chosen

    deltas = [pick([order[0][turn] for order in orders]) for turn in range(chunks)]

    def pairs_of(turn):
        delta = deltas[turn]
        for holder in range(2):
            for leaf in range(per_device):
                other = ((chip + delta) * 2 + holder) * per_device + leaf
                column = pl.multiple_of((other % CHILDREN) * RANK, RANK)
                yield holder, leaf, slot_of(delta, holder), other, other // CHILDREN - low, column

    def keep(turn, values):
        for (other, row, column, mine), act in values:
            if turn in (3, 4):
                apart = other - number - mine
                pl.when((apart <= REACH) & (apart >= -REACH))(lambda: act(row, column, mine))
            else:
                act(row, column, mine)

    def first_half(turn):
        for leaf in parts(0):
            relayed(0, deltas[turn], leaf).wait_recv()
        coupled = {}
        targets_of = {}
        for holder, leaf, slot, other, row, column in pairs_of(turn):
            left = []
            for mine in range(per_device):
                n = lookup[mine, other - number - mine + reach // 2, 0]
                left.append(halves[mine, n])
                targets_of[holder, leaf, mine] = (other, row, column, mine)
            both = matmul(jnp.concatenate(left, axis=0), win_bases[slot, leaf])
            for mine in range(per_device):
                part = both[mine * 2 * RANK : (mine + 1) * 2 * RANK]
                high, low_part = split(part[red:, :red])
                here_rows = pl.ds(mine * RANK, RANK)
                lefts[turn, holder, leaf, here_rows, :red] = high
                lefts[turn, holder, leaf, here_rows, red:] = low_part
                coupled[holder, leaf, mine] = (split(part[:red, red:]), part[red:, red:])
        kept = []
        for holder in range(2):
            for mine in range(per_device):
                tall = [
                    jnp.concatenate(coupled[holder, leaf, mine][0], axis=0)
                    for leaf in range(per_device)
                ]
                moved = matmul(turned[mine], jnp.concatenate(tall, axis=1))
                for leaf in range(per_device):
                    value = coupled[holder, leaf, mine][1] + moved[:, leaf * RANK : (leaf + 1) * RANK]

                    def act(row, column, mine, value=value):
                        blocks[mine, row, :, pl.ds(column, RANK)] = value

                    kept.append((targets_of[holder, leaf, mine], act))
        keep(turn, kept)

    def second_half(turn):
        for leaf in parts(1):
            relayed(1, deltas[turn], leaf).wait_recv()
        kept = []
        for holder, leaf, slot, other, row, column in pairs_of(turn):
            moved = win_shift[slot, leaf]
            both = matmul(lefts[turn, holder, leaf], jnp.concatenate([moved, moved], axis=0))
            for mine in range(per_device):
                value = both[mine * RANK : (mine + 1) * RANK]

                def act(row, column, mine, value=value):
                    spot = blocks[mine, row, :, pl.ds(column, RANK)]
                    blocks[mine, row, :, pl.ds(column, RANK)] = spot - value

                kept.append(((other, row, column, mine), act))
        keep(turn, kept)

    def run(half, turn):
        pl.when(exists(deltas[turn]))(lambda: half(turn))

    def row_copy(t):
        other = (seat + t) % size
        width = per_device * RANK
        return pltpu.make_async_remote_copy(
            src_ref=diagonal.at[:, :, pl.ds(pl.multiple_of(other * width, 128), width)],
            dst_ref=landed.at[size - t],
            send_sem=row_send.at[t],
            recv_sem=row_recv.at[size - t],
            device_id=(me - seat + other,),
            device_id_type=MESH,
        )

    serve(0, 3)
    for copy in fetches:
        copy.wait()
    table.wait()
    for turn in range(slots // unroll):
        project(turn)
    for turn in range(2):
        run(first_half, turn)
    serve(1, 1)
    serve(0, 4)
    for turn in range(2):
        run(second_half, turn)
    finish_factor(factor, panel, skeleton, rows, low_corner)
    for leaf in range(per_device):
        column = pl.multiple_of(((number + leaf) % CHILDREN) * RANK, RANK)
        blocks[leaf, home, :, pl.ds(column, RANK)] = skeleton[leaf]
    for leaf in range(per_device):
        diagonal[leaf] = blocks[leaf, home].astype(jnp.bfloat16)
    for t in range(1, size):
        row_copy(t).start()
    for turn in range(2, 5):
        run(first_half, turn)
    serve(1, 2)
    for turn in range(2, 5):
        run(second_half, turn)
    for step in range(5, STEPS[0] + 1):
        serve(0, step)
    for turn in range(5, chunks):
        run(first_half, turn)
    for step in range(3, STEPS[1] + 1):
        serve(1, step)
    for turn in range(5, chunks):
        run(second_half, turn)

    finish(0)
    finish(1)
    for t in range(1, size):
        row_copy(size - t).wait_recv()
    for t in range(1, size):
        row_copy(t).wait_send()


def place_kernel(
    parents, factor, panel, blocks, landed, factor_out, panel_out, merged, block_out, block, sems
):
    per_device, targets = blocks.shape[0], blocks.shape[1]
    size = landed.shape[0]
    width = per_device * RANK
    me = lax.axis_index("leaf")
    seat = me % size
    parent = me * per_device // CHILDREN
    low = jnp.clip(parent - targets // 2, 0, parents.shape[0] - targets)
    copies = []

    def put(source, target):
        copy = pltpu.make_async_copy(source, target, sems.at[len(copies)])
        copy.start()
        copies.append(copy)

    for q in range(targets):
        row = parents[parent, q] - low
        for leaf in range(per_device):
            put(blocks.at[leaf, row], merged.at[leaf, q])
    put(factor, factor_out)
    put(panel, panel_out)
    for t in range(size):
        columns = pl.ds(pl.multiple_of(((seat + t) % size) * width, 128), width)
        mine = blocks[:, parent - low, :, columns].reshape(width, width)
        if t == 0:
            theirs = mine
        else:
            theirs = landed[t].reshape(width, width).astype(jnp.float32)
        block[:, columns] = 0.5 * (mine + theirs.T)
        put(block.at[:, columns], block_out.at[:, columns])
    for copy in copies:
        copy.wait()


def local(count, near_blocks, diag_blocks, bases, leaf_nbrs, parent_nbrs):
    per_device, leaf_rows = bases.shape[0], bases.shape[1]
    red = leaf_rows - RANK
    slots = near_blocks.shape[1]
    parents, targets = parent_nbrs.shape
    assert per_device == 2 and REACH == 4 * PLANE
    vmem = pl.BlockSpec(memory_space=pltpu.VMEM)
    smem = pl.BlockSpec(memory_space=pltpu.SMEM)
    hbm = pl.BlockSpec(memory_space=pltpu.HBM)
    f32, bf16 = jnp.float32, jnp.bfloat16

    def in_hbm(array):
        return pltpu.with_memory_space_constraint(array, pltpu.HBM)

    def out(shape, dtype):
        return jax.ShapeDtypeStruct(shape, dtype)

    reach = 2 * (REACH + CHILDREN)
    size = CHILDREN // per_device
    width = per_device * RANK
    window = 2 * (2 * PLANE + 1)
    links = max(len(out_[link]) for kind in OUTBOUND for out_ in kind for link in LINKS)
    sems = pltpu.SemaphoreType.DMA
    factor, panel, blocks, landed = pl.pallas_call(
        functools.partial(level_kernel, count, parents, targets),
        out_shape=(
            out((per_device, red, red), f32),
            out((per_device, red, RANK), f32),
            out((per_device, targets, RANK, CHILDREN * RANK), f32),
            out((size, per_device, RANK, width), bf16),
        ),
        in_specs=[hbm] * 4,
        out_specs=(vmem,) * 4,
        scratch_shapes=[
            pltpu.VMEM((window,) + bases.shape, bf16),
            pltpu.VMEM((window, per_device, red, RANK), bf16),
            pltpu.VMEM(diag_blocks.shape, bf16),
            pltpu.VMEM(leaf_nbrs.shape, jnp.int32),
            pltpu.VMEM((per_device, RANK, RANK), f32),
            pltpu.VMEM((per_device, RANK, RANK), f32),
            pltpu.VMEM((per_device, RANK, 2 * red), bf16),
            pltpu.VMEM(bases.shape, bf16),
            pltpu.VMEM((per_device, red, 2 * red + RANK), f32),
            pltpu.VMEM((per_device, red, 2 * red + RANK), f32),
            pltpu.VMEM(near_blocks.shape, bf16),
            pltpu.VMEM((per_device, slots + 1) + near_blocks.shape[2:], bf16),
            pltpu.VMEM((2 * PLANE + 1, 2, per_device, per_device * RANK, 2 * red), bf16),
            pltpu.VMEM((per_device, RANK, CHILDREN * RANK), bf16),
            sems((2, len(LINKS), links)),
            sems((2, 2 * PLANE + 1, per_device)),
            sems((2, 2 * PLANE + 1, per_device)),
            sems((2, 2 * PLANE + 1, per_device)),
            sems((3,)),
            sems((per_device,)),
            sems((size,)),
            sems((size,)),
            pltpu.VMEM((per_device, reach, 128), jnp.int32),
            pltpu.SMEM((per_device, reach, 128), jnp.int32),
            sems(()),
        ],
        compiler_params=pltpu.CompilerParams(
            collective_id=0, has_side_effects=True, vmem_limit_bytes=46_500_000
        ),
        name="level",
    )(*(in_hbm(array) for array in (leaf_nbrs, diag_blocks, bases, near_blocks)))

    return pl.pallas_call(
        place_kernel,
        out_shape=(
            out((per_device, red, red), f32),
            out((per_device, red, RANK), f32),
            out((per_device, targets, RANK, CHILDREN * RANK), f32),
            out((width, CHILDREN * RANK), f32),
        ),
        in_specs=[smem, vmem, vmem, vmem, vmem],
        out_specs=(hbm,) * 4,
        scratch_shapes=[
            pltpu.VMEM((width, CHILDREN * RANK), f32),
            sems((targets * per_device + 2 + size,)),
        ],
        compiler_params=pltpu.CompilerParams(vmem_limit_bytes=16_000_000),
        name="place",
    )(parent_nbrs, factor, panel, blocks, landed)


def solution(mesh):
    count = mesh.shape["leaf"]
    in_specs = (
        P("leaf", None, None, None),
        P("leaf", None, None),
        P("leaf", None, None),
        P("leaf", None),
        P(),
    )
    out_specs = (
        P("leaf", None, None),
        P("leaf", None, None),
        P("leaf", None, None, None),
        P("leaf", None),
    )
    return jax.shard_map(
        functools.partial(local, count),
        mesh=mesh,
        in_specs=in_specs,
        out_specs=out_specs,
        check_vma=False,
    )
```

```python
import functools

import jax
import jax.numpy as jnp
from jax import lax
from jax.experimental import pallas as pl
from jax.experimental.pallas import tpu as pltpu
from jax.sharding import PartitionSpec as P

RANK = 128
REACH = 16
CHILDREN = 8
PANEL = 32
GROUP = 8
LANES = 128
PLANE = 4
LINKS = ("x", "y", "up", "down")
MESH = pl.DeviceIdType.MESH
highest = lax.Precision.HIGHEST


def matmul(a, b):
    return jnp.dot(a, b, preferred_element_type=jnp.float32)


def matmul_t(a, b, precision=None):
    return lax.dot_general(
        a, b, (((0,), (0,)), ((), ())), preferred_element_type=jnp.float32, precision=precision
    )


def halves_of(plane, chip):
    return [(plane, chip, 0), (plane, chip, 1)]


def whole(plane, chip):
    return [(plane, chip, None)]


BASES_IN = (
    {
        "x": halves_of(0, 1) + [(0, 3, 0), (-1, 1, 0)],
        "y": halves_of(0, 2) + [(0, 3, 1)] + halves_of(-1, 2),
        "up": halves_of(-1, 0) + [(-1, 1, 1)] + halves_of(-1, 3),
        "down": halves_of(1, 0),
    },
    {
        "x": halves_of(0, 0) + halves_of(0, 2),
        "y": halves_of(0, 3) + halves_of(-1, 3),
        "up": halves_of(-1, 1) + halves_of(-1, 2),
        "down": halves_of(1, 1) + halves_of(1, 0),
    },
    {
        "x": halves_of(0, 3) + halves_of(0, 1),
        "y": halves_of(0, 0) + halves_of(1, 0),
        "up": halves_of(-1, 2) + halves_of(-1, 3),
        "down": halves_of(1, 2) + halves_of(1, 1),
    },
    {
        "x": halves_of(0, 2) + [(0, 0, 0), (1, 2, 0)],
        "y": halves_of(0, 1) + [(0, 0, 1)] + halves_of(1, 1),
        "up": halves_of(-1, 3),
        "down": halves_of(1, 3) + [(1, 2, 1)] + halves_of(1, 0),
    },
)
SHIFTS_IN = (
    {
        "x": whole(0, 1) + whole(-1, 1),
        "y": whole(0, 2) + whole(0, 3) + whole(-1, 2),
        "up": whole(-1, 0) + whole(-1, 3),
        "down": whole(1, 0),
    },
    {
        "x": whole(0, 0) + whole(0, 2),
        "y": whole(0, 3) + whole(-1, 3),
        "up": whole(-1, 1) + whole(-1, 2),
        "down": whole(1, 1) + whole(1, 0),
    },
    {
        "x": whole(0, 3) + whole(0, 1),
        "y": whole(0, 0) + whole(1, 0),
        "up": whole(-1, 2) + whole(-1, 3),
        "down": whole(1, 2) + whole(1, 1),
    },
    {
        "x": whole(0, 2) + whole(1, 2),
        "y": whole(0, 1) + whole(0, 0) + whole(1, 1),
        "up": whole(-1, 3),
        "down": whole(1, 3) + whole(1, 0),
    },
)


def plan(inbound):
    outbound = []
    for place in range(PLANE):
        out = {"x": inbound[place ^ 1]["x"], "y": inbound[place ^ 2]["y"]}
        out["up"] = [(plane + 1, chip, leaf) for plane, chip, leaf in inbound[place]["up"]]
        out["down"] = [(plane - 1, chip, leaf) for plane, chip, leaf in inbound[place]["down"]]
        outbound.append(out)
    held = [{(0, place, leaf): 0 for leaf in (0, 1, None)} for place in range(PLANE)]
    arrivals = [[] for _ in range(PLANE)]
    queue = {(place, link): 0 for place in range(PLANE) for link in LINKS}
    now = 0
    while any(queue[place, link] < len(outbound[place][link]) for place, link in queue):
        now += 1
        landed = []
        for (place, link), done in queue.items():
            items = outbound[place][link]
            if done < len(items) and held[place].get(items[done], now) < now:
                target = {"x": place ^ 1, "y": place ^ 2}.get(link, place)
                landed.append((target, inbound[target][link][done]))
                queue[place, link] = done + 1
        for target, item in landed:
            held[target][item] = now
            arrivals[target].append((now, item))
    return outbound, arrivals, now


OUTBOUND, ARRIVALS, STEPS = zip(plan(BASES_IN), plan(SHIFTS_IN))


def shift_of(place, item):
    plane, chip, _ = item
    return PLANE * plane + chip - place


def chunk_order(place):
    ready = [{0: 0}, {0: 0}]
    for kind in range(2):
        for now, item in ARRIVALS[kind][place]:
            ready[kind][shift_of(place, item)] = now
    first = [0, (place ^ 1) - place, (place ^ 2) - place, -PLANE, PLANE]
    rest = sorted((ready[1][delta], now, delta) for delta, now in ready[0].items() if delta not in first)
    order = first + [delta for _, _, delta in rest]
    return order, [(ready[0][delta], ready[1][delta]) for delta in order]


def reduce_blocks(diag, bases, bases_t, work, low_corner):
    per_device, leaf_rows = bases.shape[0], bases.shape[1]
    red = leaf_rows - RANK
    row_id = lax.broadcasted_iota(jnp.int32, (red, red), 0)
    col_id = lax.broadcasted_iota(jnp.int32, (red, red), 1)
    for leaf in range(per_device):
        basis = bases[leaf]
        basis_t = basis.T
        bases_t[leaf] = basis_t
        half = matmul(basis_t, diag[leaf]).astype(jnp.bfloat16)
        dense = matmul(half, basis)
        top = dense[:red, :red]
        work[leaf, :, :red] = 0.5 * (top + top.T)
        work[leaf, :, red : red + RANK] = dense[:red, red:]
        work[leaf, :, red + RANK :] = (row_id == col_id).astype(jnp.float32)
        low_corner[leaf] = dense[red:, red:]


def eliminate(shift, turned, work, rows, serve):
    per_device, red = work.shape[0], work.shape[1]
    tiles = work.shape[2] // LANES
    row_id = lax.broadcasted_iota(jnp.int32, (red, red), 0)
    col_id = lax.broadcasted_iota(jnp.int32, (red, red), 1)
    sub = lax.broadcasted_iota(jnp.int32, (GROUP, LANES), 0)
    groups = PANEL // GROUP
    leaves = range(per_device)
    for start in range(0, red, PANEL):
        strips = [
            [
                [
                    work[leaf, pl.ds(start + GROUP * v, GROUP), pl.ds(LANES * t, LANES)]
                    for t in range(tiles)
                ]
                for v in range(groups)
            ]
            for leaf in leaves
        ]
        for g in range(groups):
            first = start + GROUP * g
            columns = [
                {
                    v: [
                        jnp.broadcast_to(strips[leaf][v][0][:, first + c : first + c + 1], (GROUP, LANES))
                        for c in range(GROUP)
                    ]
                    for v in range(g, groups)
                }
                for leaf in leaves
            ]
            for r in range(GROUP):
                for leaf in leaves:
                    cols, strip = columns[leaf], strips[leaf]
                    inverse = 1.0 / cols[g][r][r : r + 1]
                    heads = [cols[g][c][r : r + 1] for c in range(GROUP)]
                    lines = [strip[g][t][r : r + 1] for t in range(tiles)]
                    for v in range(g, groups):
                        ratio = cols[v][r] * inverse
                        if v == g:
                            ratio = jnp.where(sub > r, ratio, 0.0)
                        for c in range(r + 1, GROUP):
                            cols[v][c] = cols[v][c] - ratio * heads[c]
                        for t in range(tiles):
                            strip[v][t] = strip[v][t] - ratio * lines[t]
            for leaf in leaves:
                pivots = columns[leaf][g][0]
                for r in range(1, GROUP):
                    pivots = jnp.where(sub == r, columns[leaf][g][r], pivots)
                scale = 1.0 / jnp.sqrt(pivots)
                for t in range(tiles):
                    here = (leaf, pl.ds(first, GROUP), pl.ds(LANES * t, LANES))
                    rows[here] = strips[leaf][g][t] * scale
        if start + PANEL < red:
            for leaf in leaves:
                strip = rows[leaf, start : start + PANEL, :]
                work[leaf] = work[leaf] - matmul_t(strip[:, :red], strip, highest)
        serve(start // PANEL)
    for leaf in range(per_device):
        solved = rows[leaf, :, red : red + RANK]
        inverse = jnp.where(col_id <= row_id, rows[leaf, :, red + RANK :], 0.0)
        moved = matmul_t(inverse, solved, highest)
        shift[leaf] = moved.astype(jnp.bfloat16)
        back = -moved.astype(jnp.bfloat16).astype(jnp.float32).T
        turned[leaf, :, :red] = back.astype(jnp.bfloat16)
        turned[leaf, :, red:] = back.astype(jnp.bfloat16)


def finish_factor(factor, panel, skeleton, rows, low_corner):
    per_device, red = rows.shape[0], rows.shape[1]
    row_id = lax.broadcasted_iota(jnp.int32, (red, red), 0)
    col_id = lax.broadcasted_iota(jnp.int32, (red, red), 1)
    for leaf in range(per_device):
        solved = rows[leaf, :, red : red + RANK]
        panel[leaf] = solved
        skeleton[leaf] = low_corner[leaf] - matmul_t(solved, solved, highest)
        upper = jnp.where(col_id >= row_id, rows[leaf, :, :red], 0.0)
        factor[leaf] = upper.T


def split(values):
    high = values.astype(jnp.bfloat16)
    return high, (values - high.astype(jnp.float32)).astype(jnp.bfloat16)


def level_kernel(
    count,
    parents,
    targets,
    nbrs,
    diag,
    bases,
    near,
    factor,
    panel,
    blocks,
    landed,
    win_bases,
    win_shift,
    diag_in,
    nbrs_in,
    low_corner,
    skeleton,
    turned,
    bases_t,
    work,
    rows,
    near_in,
    halves,
    lefts,
    diagonal,
    send,
    recv,
    pass_send,
    pass_recv,
    in_sem,
    near_sem,
    row_send,
    row_recv,
    found,
    lookup,
    found_sem,
):
    per_device, slots = near_in.shape[0], near_in.shape[1]
    red = rows.shape[1]
    total = count // 2
    me = lax.axis_index("leaf")
    core, chip = me % 2, me // 2
    sibling = me + 1 - 2 * core
    place = chip % PLANE
    size = CHILDREN // per_device
    seat = me % size
    across = me + 2 * (1 - 2 * (place % 2))
    along = me + 4 * (1 - 2 * (place // 2))
    device = {"x": across, "y": along, "up": me + 2 * PLANE, "down": me - 2 * PLANE}
    present = {"up": chip + PLANE < total, "down": chip - PLANE >= 0}
    far = across + 1 - 2 * core

    fetches = [
        pltpu.make_async_copy(near.at[leaf], near_in.at[leaf], near_sem.at[leaf])
        for leaf in range(per_device)
    ]
    here = 2 * PLANE + core
    inputs = [
        pltpu.make_async_copy(source, target, in_sem.at[n])
        for n, (source, target) in enumerate(
            ((nbrs, nbrs_in), (bases, win_bases.at[here]), (diag, diag_in))
        )
    ]
    for copy in inputs + fetches:
        copy.start()

    barrier = pltpu.get_barrier_semaphore()
    for other in (sibling, across, along, far):
        pl.semaphore_signal(barrier, inc=1, device_id=(other,), device_id_type=MESH)
    peers = jnp.int32(4)
    for link in ("up", "down"):

        @pl.when(present[link])
        def _(link=link):
            pl.semaphore_signal(barrier, inc=1, device_id=(device[link],), device_id_type=MESH)

        peers = peers + present[link].astype(jnp.int32)

    windows = (win_bases, win_shift)

    def exists(delta):
        return (chip + delta >= 0) & (chip + delta < total)

    def slot_of(delta, holder):
        return 2 * (PLANE + delta) + holder

    def block_of(kind, delta, holder, leaf):
        block = windows[kind].at[slot_of(delta, holder)]
        return block if leaf is None else block.at[leaf]

    def hop(kind, at, link, order):
        item = OUTBOUND[kind][at][link][order]
        delta, leaf = shift_of(at, item), item[2]
        moved = {"x": at - (at ^ 1), "y": at - (at ^ 2), "up": -PLANE, "down": PLANE}[link]
        return pltpu.make_async_remote_copy(
            src_ref=block_of(kind, delta, core, leaf),
            dst_ref=block_of(kind, delta + moved, core, leaf),
            send_sem=send.at[kind, LINKS.index(link), order],
            recv_sem=recv.at[kind, PLANE + delta + moved, leaf or 0],
            device_id=(device[link],),
            device_id_type=MESH,
        )

    def arrival(kind, delta, leaf):
        there = block_of(kind, delta, core, leaf)
        return pltpu.make_async_remote_copy(
            src_ref=there,
            dst_ref=there,
            send_sem=send.at[kind, 0, 0],
            recv_sem=recv.at[kind, PLANE + delta, leaf or 0],
            device_id=(sibling,),
            device_id_type=MESH,
        )

    def relay(kind, delta, leaf):
        there = block_of(kind, delta, core, leaf)
        return pltpu.make_async_remote_copy(
            src_ref=there,
            dst_ref=there,
            send_sem=pass_send.at[kind, PLANE + delta, leaf or 0],
            recv_sem=pass_recv.at[kind, PLANE + delta, leaf or 0],
            device_id=(sibling,),
            device_id_type=MESH,
        )

    def relayed(kind, delta, leaf):
        there = block_of(kind, delta, 1 - core, leaf)
        return pltpu.make_async_remote_copy(
            src_ref=there,
            dst_ref=there,
            send_sem=pass_send.at[kind, PLANE + delta, leaf or 0],
            recv_sem=pass_recv.at[kind, PLANE + delta, leaf or 0],
            device_id=(sibling,),
            device_id_type=MESH,
        )

    def parts(kind):
        return (None,) if kind else range(per_device)

    def on_links(kind, at, item, act):
        for link in LINKS:
            for order, entry in enumerate(OUTBOUND[kind][at][link]):
                if entry == item:
                    if link in present:
                        pl.when(present[link])(lambda: act(hop(kind, at, link, order)))
                    else:
                        act(hop(kind, at, link, order))

    def start(copy):
        copy.start()

    def stop(copy):
        copy.wait_send()

    def by_place(act):
        for at in range(PLANE):
            pl.when(place == at)(lambda: act(at))

    def dispatch(kind):
        def act(at):
            for leaf in parts(kind):
                on_links(kind, at, (0, at, leaf), start)

        by_place(act)
        for leaf in parts(kind):
            relay(kind, 0, leaf).start()

    def serve(kind, step):
        def act(at):
            for now, item in ARRIVALS[kind][at]:
                if now == step:
                    delta, leaf = shift_of(at, item), item[2]

                    def one():
                        arrival(kind, delta, leaf).wait_recv()
                        on_links(kind, at, item, start)
                        relay(kind, delta, leaf).start()

                    if item[0] == 0:
                        one()
                    else:
                        pl.when(exists(delta))(one)

        by_place(act)

    def finish(kind):
        def act(at):
            for leaf in parts(kind):
                on_links(kind, at, (0, at, leaf), stop)
            for _, item in ARRIVALS[kind][at]:
                delta, leaf = shift_of(at, item), item[2]

                def one():
                    on_links(kind, at, item, stop)
                    relay(kind, delta, leaf).wait_send()

                if item[0] == 0:
                    one()
                else:
                    pl.when(exists(delta))(one)

        by_place(act)
        for leaf in parts(kind):
            relay(kind, 0, leaf).wait_send()

    number = me * per_device
    parent = number // CHILDREN
    low = jnp.clip(parent - targets // 2, 0, parents - targets)
    home = parent - low
    inputs[1].wait()
    pl.semaphore_wait(barrier, peers)
    dispatch(0)
    inputs[2].wait()
    reduce_blocks(diag_in, win_bases.at[here], bases_t, work, low_corner)

    def between(panel_done):
        if panel_done > 0 and panel_done < red // PANEL - 1:
            serve(0, panel_done)

    eliminate(win_shift.at[here], turned, work, rows, between)
    dispatch(1)
    blocks[...] = jnp.zeros_like(blocks)
    halves[:, slots] = jnp.zeros_like(halves[:, slots])
    reach = found.shape[1]
    offset = lax.broadcasted_iota(jnp.int32, (reach, slots), 0) - reach // 2
    order = lax.broadcasted_iota(jnp.int32, (reach, slots), 1)
    inputs[0].wait()
    for leaf in range(per_device):
        away = offset + number + leaf
        hit = (nbrs_in[leaf : leaf + 1, :] == away) & (away >= 0)
        slot = jnp.max(jnp.where(hit, order, -1), axis=1, keepdims=True)
        found[leaf] = jnp.broadcast_to(jnp.where(slot < 0, slots, slot), found.shape[1:])
    table = pltpu.make_async_copy(found, lookup, found_sem)
    table.start()

    unroll = max(n for n in range(1, 14) if slots % n == 0)

    def project(turn):
        for k in range(unroll):
            n = turn * unroll + k
            for leaf in range(per_device):
                halves[leaf, n] = matmul(bases_t[leaf], near_in[leaf, n]).astype(jnp.bfloat16)

    orders = [chunk_order(at) for at in range(PLANE)]
    chunks = len(orders[0][0])

    def pick(values):
        chosen = jnp.int32(values[0])
        for at in range(1, PLANE):
            chosen = jnp.where(place == at, jnp.int32(values[at]), chosen)
        return chosen

    deltas = [pick([order[0][turn] for order in orders]) for turn in range(chunks)]

    def pairs_of(turn):
        delta = deltas[turn]
        for holder in range(2):
            for leaf in range(per_device):
                other = ((chip + delta) * 2 + holder) * per_device + leaf
                column = pl.multiple_of((other % CHILDREN) * RANK, RANK)
                yield holder, leaf, slot_of(delta, holder), other, other // CHILDREN - low, column

    def keep(turn, values):
        for (other, row, column, mine), act in values:
            if turn in (3, 4):
                apart = other - number - mine
                pl.when((apart <= REACH) & (apart >= -REACH))(lambda: act(row, column, mine))
            else:
                act(row, column, mine)

    def first_half(turn):
        for leaf in parts(0):
            relayed(0, deltas[turn], leaf).wait_recv()
        coupled = {}
        targets_of = {}
        for holder, leaf, slot, other, row, column in pairs_of(turn):
            left = []
            for mine in range(per_device):
                n = lookup[mine, other - number - mine + reach // 2, 0]
                left.append(halves[mine, n])
                targets_of[holder, leaf, mine] = (other, row, column, mine)
            both = matmul(jnp.concatenate(left, axis=0), win_bases[slot, leaf])
            for mine in range(per_device):
                part = both[mine * 2 * RANK : (mine + 1) * 2 * RANK]
                high, low_part = split(part[red:, :red])
                here_rows = pl.ds(mine * RANK, RANK)
                lefts[turn, holder, leaf, here_rows, :red] = high
                lefts[turn, holder, leaf, here_rows, red:] = low_part
                coupled[holder, leaf, mine] = (split(part[:red, red:]), part[red:, red:])
        kept = []
        for holder in range(2):
            for mine in range(per_device):
                tall = [
                    jnp.concatenate(coupled[holder, leaf, mine][0], axis=0)
                    for leaf in range(per_device)
                ]
                moved = matmul(turned[mine], jnp.concatenate(tall, axis=1))
                for leaf in range(per_device):
                    value = coupled[holder, leaf, mine][1] + moved[:, leaf * RANK : (leaf + 1) * RANK]

                    def act(row, column, mine, value=value):
                        blocks[mine, row, :, pl.ds(column, RANK)] = value

                    kept.append((targets_of[holder, leaf, mine], act))
        keep(turn, kept)

    def second_half(turn):
        for leaf in parts(1):
            relayed(1, deltas[turn], leaf).wait_recv()
        kept = []
        for holder, leaf, slot, other, row, column in pairs_of(turn):
            moved = win_shift[slot, leaf]
            both = matmul(lefts[turn, holder, leaf], jnp.concatenate([moved, moved], axis=0))
            for mine in range(per_device):
                value = both[mine * RANK : (mine + 1) * RANK]

                def act(row, column, mine, value=value):
                    spot = blocks[mine, row, :, pl.ds(column, RANK)]
                    blocks[mine, row, :, pl.ds(column, RANK)] = spot - value

                kept.append(((other, row, column, mine), act))
        keep(turn, kept)

    def run(half, turn):
        pl.when(exists(deltas[turn]))(lambda: half(turn))

    def row_copy(t):
        other = (seat + t) % size
        width = per_device * RANK
        return pltpu.make_async_remote_copy(
            src_ref=diagonal.at[:, :, pl.ds(pl.multiple_of(other * width, 128), width)],
            dst_ref=landed.at[size - t],
            send_sem=row_send.at[t],
            recv_sem=row_recv.at[size - t],
            device_id=(me - seat + other,),
            device_id_type=MESH,
        )

    serve(0, 3)
    for copy in fetches:
        copy.wait()
    table.wait()
    for turn in range(slots // unroll):
        project(turn)
    for turn in range(2):
        run(first_half, turn)
    serve(1, 1)
    serve(0, 4)
    for turn in range(2):
        run(second_half, turn)
    finish_factor(factor, panel, skeleton, rows, low_corner)
    for leaf in range(per_device):
        column = pl.multiple_of(((number + leaf) % CHILDREN) * RANK, RANK)
        blocks[leaf, home, :, pl.ds(column, RANK)] = skeleton[leaf]
    for leaf in range(per_device):
        diagonal[leaf] = blocks[leaf, home].astype(jnp.bfloat16)
    for t in range(1, size):
        row_copy(t).start()
    for turn in range(2, 5):
        run(first_half, turn)
    serve(1, 2)
    for turn in range(2, 5):
        run(second_half, turn)
    for step in range(5, STEPS[0] + 1):
        serve(0, step)
    for turn in range(5, chunks):
        run(first_half, turn)
    for step in range(3, STEPS[1] + 1):
        serve(1, step)
    for turn in range(5, chunks):
        run(second_half, turn)

    finish(0)
    finish(1)
    for t in range(1, size):
        row_copy(size - t).wait_recv()
    for t in range(1, size):
        row_copy(t).wait_send()


def place_kernel(
    parents, factor, panel, blocks, landed, factor_out, panel_out, merged, block_out, block, sems
):
    per_device, targets = blocks.shape[0], blocks.shape[1]
    size = landed.shape[0]
    width = per_device * RANK
    me = lax.axis_index("leaf")
    seat = me % size
    parent = me * per_device // CHILDREN
    low = jnp.clip(parent - targets // 2, 0, parents.shape[0] - targets)
    copies = []

    def put(source, target):
        copy = pltpu.make_async_copy(source, target, sems.at[len(copies)])
        copy.start()
        copies.append(copy)

    for q in range(targets):
        row = parents[parent, q] - low
        for leaf in range(per_device):
            put(blocks.at[leaf, row], merged.at[leaf, q])
    put(factor, factor_out)
    put(panel, panel_out)
    for t in range(size):
        columns = pl.ds(pl.multiple_of(((seat + t) % size) * width, 128), width)
        mine = blocks[:, parent - low, :, columns].reshape(width, width)
        if t == 0:
            theirs = mine
        else:
            theirs = landed[t].reshape(width, width).astype(jnp.float32)
        block[:, columns] = 0.5 * (mine + theirs.T)
        put(block.at[:, columns], block_out.at[:, columns])
    for copy in copies:
        copy.wait()


def local(count, near_blocks, diag_blocks, bases, leaf_nbrs, parent_nbrs):
    per_device, leaf_rows = bases.shape[0], bases.shape[1]
    red = leaf_rows - RANK
    slots = near_blocks.shape[1]
    parents, targets = parent_nbrs.shape
    assert per_device == 2 and REACH == 4 * PLANE
    vmem = pl.BlockSpec(memory_space=pltpu.VMEM)
    smem = pl.BlockSpec(memory_space=pltpu.SMEM)
    hbm = pl.BlockSpec(memory_space=pltpu.HBM)
    f32, bf16 = jnp.float32, jnp.bfloat16

    def in_hbm(array):
        return pltpu.with_memory_space_constraint(array, pltpu.HBM)

    def out(shape, dtype):
        return jax.ShapeDtypeStruct(shape, dtype)

    reach = 2 * (REACH + CHILDREN)
    size = CHILDREN // per_device
    width = per_device * RANK
    window = 2 * (2 * PLANE + 1)
    links = max(len(out_[link]) for kind in OUTBOUND for out_ in kind for link in LINKS)
    sems = pltpu.SemaphoreType.DMA
    factor, panel, blocks, landed = pl.pallas_call(
        functools.partial(level_kernel, count, parents, targets),
        out_shape=(
            out((per_device, red, red), f32),
            out((per_device, red, RANK), f32),
            out((per_device, targets, RANK, CHILDREN * RANK), f32),
            out((size, per_device, RANK, width), bf16),
        ),
        in_specs=[hbm] * 4,
        out_specs=(vmem,) * 4,
        scratch_shapes=[
            pltpu.VMEM((window,) + bases.shape, bf16),
            pltpu.VMEM((window, per_device, red, RANK), bf16),
            pltpu.VMEM(diag_blocks.shape, bf16),
            pltpu.VMEM(leaf_nbrs.shape, jnp.int32),
            pltpu.VMEM((per_device, RANK, RANK), f32),
            pltpu.VMEM((per_device, RANK, RANK), f32),
            pltpu.VMEM((per_device, RANK, 2 * red), bf16),
            pltpu.VMEM(bases.shape, bf16),
            pltpu.VMEM((per_device, red, 2 * red + RANK), f32),
            pltpu.VMEM((per_device, red, 2 * red + RANK), f32),
            pltpu.VMEM(near_blocks.shape, bf16),
            pltpu.VMEM((per_device, slots + 1) + near_blocks.shape[2:], bf16),
            pltpu.VMEM((2 * PLANE + 1, 2, per_device, per_device * RANK, 2 * red), bf16),
            pltpu.VMEM((per_device, RANK, CHILDREN * RANK), bf16),
            sems((2, len(LINKS), links)),
            sems((2, 2 * PLANE + 1, per_device)),
            sems((2, 2 * PLANE + 1, per_device)),
            sems((2, 2 * PLANE + 1, per_device)),
            sems((3,)),
            sems((per_device,)),
            sems((size,)),
            sems((size,)),
            pltpu.VMEM((per_device, reach, 128), jnp.int32),
            pltpu.SMEM((per_device, reach, 128), jnp.int32),
            sems(()),
        ],
        compiler_params=pltpu.CompilerParams(
            collective_id=0, has_side_effects=True, vmem_limit_bytes=46_500_000
        ),
        name="level",
    )(*(in_hbm(array) for array in (leaf_nbrs, diag_blocks, bases, near_blocks)))

    return pl.pallas_call(
        place_kernel,
        out_shape=(
            out((per_device, red, red), f32),
            out((per_device, red, RANK), f32),
            out((per_device, targets, RANK, CHILDREN * RANK), f32),
            out((width, CHILDREN * RANK), f32),
        ),
        in_specs=[smem, vmem, vmem, vmem, vmem],
        out_specs=(hbm,) * 4,
        scratch_shapes=[
            pltpu.VMEM((width, CHILDREN * RANK), f32),
            sems((targets * per_device + 2 + size,)),
        ],
        compiler_params=pltpu.CompilerParams(vmem_limit_bytes=16_000_000),
        name="place",
    )(parent_nbrs, factor, panel, blocks, landed)


def solution(mesh):
    count = mesh.shape["leaf"]
    in_specs = (
        P("leaf", None, None, None),
        P("leaf", None, None),
        P("leaf", None, None),
        P("leaf", None),
        P(),
    )
    out_specs = (
        P("leaf", None, None),
        P("leaf", None, None),
        P("leaf", None, None, None),
        P("leaf", None),
    )
    return jax.shard_map(
        functools.partial(local, count),
        mesh=mesh,
        in_specs=in_specs,
        out_specs=out_specs,
        check_vma=False,
    )
```

```python
import functools

import jax
import jax.numpy as jnp
from jax import lax
from jax.experimental import pallas as pl
from jax.experimental.pallas import tpu as pltpu
from jax.sharding import PartitionSpec as P

RANK = 128
REACH = 16
CHILDREN = 8
PANEL = 32
GROUP = 8
LANES = 128
PLANE = 4
LINKS = ("x", "y", "up", "down")
MESH = pl.DeviceIdType.MESH
highest = lax.Precision.HIGHEST


def matmul(a, b):
    return jnp.dot(a, b, preferred_element_type=jnp.float32)


def matmul_t(a, b, precision=None):
    return lax.dot_general(
        a, b, (((0,), (0,)), ((), ())), preferred_element_type=jnp.float32, precision=precision
    )


def halves_of(plane, chip):
    return [(plane, chip, 0), (plane, chip, 1)]


def whole(plane, chip):
    return [(plane, chip, None)]


BASES_IN = (
    {
        "x": halves_of(0, 1) + [(0, 3, 0), (-1, 1, 0)],
        "y": halves_of(0, 2) + [(0, 3, 1)] + halves_of(-1, 2),
        "up": halves_of(-1, 0) + [(-1, 1, 1)] + halves_of(-1, 3),
        "down": halves_of(1, 0),
    },
    {
        "x": halves_of(0, 0) + [(0, 2, 0)],
        "y": halves_of(0, 3) + [(0, 2, 1), (-1, 3, 0)],
        "up": halves_of(-1, 1) + [(-1, 3, 1)] + halves_of(-1, 2),
        "down": halves_of(1, 1) + halves_of(1, 0),
    },
    {
        "x": halves_of(0, 3) + [(0, 1, 0)],
        "y": halves_of(0, 0) + [(0, 1, 1), (1, 0, 0)],
        "up": halves_of(-1, 2) + halves_of(-1, 3),
        "down": halves_of(1, 2) + [(1, 0, 1)] + halves_of(1, 1),
    },
    {
        "x": halves_of(0, 2) + [(0, 0, 0), (1, 2, 0)],
        "y": halves_of(0, 1) + [(0, 0, 1)] + halves_of(1, 1),
        "up": halves_of(-1, 3),
        "down": halves_of(1, 3) + [(1, 2, 1)] + halves_of(1, 0),
    },
)
SHIFTS_IN = (
    {
        "x": whole(0, 1) + whole(-1, 1),
        "y": whole(0, 2) + whole(0, 3) + whole(-1, 2),
        "up": whole(-1, 0) + whole(-1, 3),
        "down": whole(1, 0),
    },
    {
        "x": whole(0, 0) + whole(0, 2),
        "y": whole(0, 3) + whole(-1, 3),
        "up": whole(-1, 1) + whole(-1, 2),
        "down": whole(1, 1) + whole(1, 0),
    },
    {
        "x": whole(0, 3) + whole(0, 1),
        "y": whole(0, 0) + whole(1, 0),
        "up": whole(-1, 2) + whole(-1, 3),
        "down": whole(1, 2) + whole(1, 1),
    },
    {
        "x": whole(0, 2) + whole(1, 2),
        "y": whole(0, 1) + whole(0, 0) + whole(1, 1),
        "up": whole(-1, 3),
        "down": whole(1, 3) + whole(1, 0),
    },
)


def plan(inbound):
    outbound = []
    for place in range(PLANE):
        out = {"x": inbound[place ^ 1]["x"], "y": inbound[place ^ 2]["y"]}
        out["up"] = [(plane + 1, chip, leaf) for plane, chip, leaf in inbound[place]["up"]]
        out["down"] = [(plane - 1, chip, leaf) for plane, chip, leaf in inbound[place]["down"]]
        outbound.append(out)
    held = [{(0, place, leaf): 0 for leaf in (0, 1, None)} for place in range(PLANE)]
    arrivals = [[] for _ in range(PLANE)]
    queue = {(place, link): 0 for place in range(PLANE) for link in LINKS}
    now = 0
    while any(queue[place, link] < len(outbound[place][link]) for place, link in queue):
        now += 1
        landed = []
        for (place, link), done in queue.items():
            items = outbound[place][link]
            if done < len(items) and held[place].get(items[done], now) < now:
                target = {"x": place ^ 1, "y": place ^ 2}.get(link, place)
                landed.append((target, inbound[target][link][done]))
                queue[place, link] = done + 1
        for target, item in landed:
            held[target][item] = now
            arrivals[target].append((now, item))
    return outbound, arrivals, now


OUTBOUND, ARRIVALS, STEPS = zip(plan(BASES_IN), plan(SHIFTS_IN))


def shift_of(place, item):
    plane, chip, _ = item
    return PLANE * plane + chip - place


def chunk_order(place):
    ready = [{0: 0}, {0: 0}]
    for kind in range(2):
        for now, item in ARRIVALS[kind][place]:
            ready[kind][shift_of(place, item)] = now
    first = [0, (place ^ 1) - place, (place ^ 2) - place, -PLANE, PLANE]
    rest = sorted((ready[1][delta], now, delta) for delta, now in ready[0].items() if delta not in first)
    order = first + [delta for _, _, delta in rest]
    return order, [(ready[0][delta], ready[1][delta]) for delta in order]


def reduce_blocks(diag, bases, bases_t, work, low_corner):
    per_device, leaf_rows = bases.shape[0], bases.shape[1]
    red = leaf_rows - RANK
    row_id = lax.broadcasted_iota(jnp.int32, (red, red), 0)
    col_id = lax.broadcasted_iota(jnp.int32, (red, red), 1)
    for leaf in range(per_device):
        basis = bases[leaf]
        basis_t = basis.T
        bases_t[leaf] = basis_t
        half = matmul(basis_t, diag[leaf]).astype(jnp.bfloat16)
        dense = matmul(half, basis)
        top = dense[:red, :red]
        work[leaf, :, :red] = 0.5 * (top + top.T)
        work[leaf, :, red : red + RANK] = dense[:red, red:]
        work[leaf, :, red + RANK :] = (row_id == col_id).astype(jnp.float32)
        low_corner[leaf] = dense[red:, red:]


def eliminate(shift, turned, work, rows, serve):
    per_device, red = work.shape[0], work.shape[1]
    tiles = work.shape[2] // LANES
    row_id = lax.broadcasted_iota(jnp.int32, (red, red), 0)
    col_id = lax.broadcasted_iota(jnp.int32, (red, red), 1)
    sub = lax.broadcasted_iota(jnp.int32, (GROUP, LANES), 0)
    groups = PANEL // GROUP
    leaves = range(per_device)
    for start in range(0, red, PANEL):
        strips = [
            [
                [
                    work[leaf, pl.ds(start + GROUP * v, GROUP), pl.ds(LANES * t, LANES)]
                    for t in range(tiles)
                ]
                for v in range(groups)
            ]
            for leaf in leaves
        ]
        for g in range(groups):
            first = start + GROUP * g
            columns = [
                {
                    v: [
                        jnp.broadcast_to(strips[leaf][v][0][:, first + c : first + c + 1], (GROUP, LANES))
                        for c in range(GROUP)
                    ]
                    for v in range(g, groups)
                }
                for leaf in leaves
            ]
            for r in range(GROUP):
                for leaf in leaves:
                    cols, strip = columns[leaf], strips[leaf]
                    inverse = 1.0 / cols[g][r][r : r + 1]
                    heads = [cols[g][c][r : r + 1] for c in range(GROUP)]
                    lines = [strip[g][t][r : r + 1] for t in range(tiles)]
                    for v in range(g, groups):
                        ratio = cols[v][r] * inverse
                        if v == g:
                            ratio = jnp.where(sub > r, ratio, 0.0)
                        for c in range(r + 1, GROUP):
                            cols[v][c] = cols[v][c] - ratio * heads[c]
                        for t in range(tiles):
                            strip[v][t] = strip[v][t] - ratio * lines[t]
            for leaf in leaves:
                pivots = columns[leaf][g][0]
                for r in range(1, GROUP):
                    pivots = jnp.where(sub == r, columns[leaf][g][r], pivots)
                scale = 1.0 / jnp.sqrt(pivots)
                for t in range(tiles):
                    here = (leaf, pl.ds(first, GROUP), pl.ds(LANES * t, LANES))
                    rows[here] = strips[leaf][g][t] * scale
        if start + PANEL < red:
            for leaf in leaves:
                strip = rows[leaf, start : start + PANEL, :]
                work[leaf] = work[leaf] - matmul_t(strip[:, :red], strip, highest)
        serve(start // PANEL)
    for leaf in range(per_device):
        solved = rows[leaf, :, red : red + RANK]
        inverse = jnp.where(col_id <= row_id, rows[leaf, :, red + RANK :], 0.0)
        moved = matmul_t(inverse, solved, highest)
        shift[leaf] = moved.astype(jnp.bfloat16)
        back = -moved.astype(jnp.bfloat16).astype(jnp.float32).T
        turned[leaf, :, :red] = back.astype(jnp.bfloat16)
        turned[leaf, :, red:] = back.astype(jnp.bfloat16)


def finish_factor(factor, panel, skeleton, rows, low_corner):
    per_device, red = rows.shape[0], rows.shape[1]
    row_id = lax.broadcasted_iota(jnp.int32, (red, red), 0)
    col_id = lax.broadcasted_iota(jnp.int32, (red, red), 1)
    for leaf in range(per_device):
        solved = rows[leaf, :, red : red + RANK]
        panel[leaf] = solved
        skeleton[leaf] = low_corner[leaf] - matmul_t(solved, solved, highest)
        upper = jnp.where(col_id >= row_id, rows[leaf, :, :red], 0.0)
        factor[leaf] = upper.T


def split(values):
    high = values.astype(jnp.bfloat16)
    return high, (values - high.astype(jnp.float32)).astype(jnp.bfloat16)


def level_kernel(
    count,
    parents,
    targets,
    nbrs,
    diag,
    bases,
    near,
    factor,
    panel,
    blocks,
    landed,
    win_bases,
    win_shift,
    diag_in,
    nbrs_in,
    low_corner,
    skeleton,
    turned,
    bases_t,
    work,
    rows,
    near_in,
    halves,
    lefts,
    diagonal,
    send,
    recv,
    pass_send,
    pass_recv,
    in_sem,
    near_sem,
    row_send,
    row_recv,
    found,
    lookup,
    found_sem,
):
    per_device, slots = near_in.shape[0], near_in.shape[1]
    red = rows.shape[1]
    total = count // 2
    me = lax.axis_index("leaf")
    core, chip = me % 2, me // 2
    sibling = me + 1 - 2 * core
    place = chip % PLANE
    size = CHILDREN // per_device
    seat = me % size
    across = me + 2 * (1 - 2 * (place % 2))
    along = me + 4 * (1 - 2 * (place // 2))
    device = {"x": across, "y": along, "up": me + 2 * PLANE, "down": me - 2 * PLANE}
    present = {"up": chip + PLANE < total, "down": chip - PLANE >= 0}
    far = across + 1 - 2 * core

    fetches = [
        pltpu.make_async_copy(near.at[leaf], near_in.at[leaf], near_sem.at[leaf])
        for leaf in range(per_device)
    ]
    here = 2 * PLANE + core
    inputs = [
        pltpu.make_async_copy(source, target, in_sem.at[n])
        for n, (source, target) in enumerate(
            ((nbrs, nbrs_in), (bases, win_bases.at[here]), (diag, diag_in))
        )
    ]
    for copy in inputs + fetches:
        copy.start()

    barrier = pltpu.get_barrier_semaphore()
    for other in (sibling, across, along, far):
        pl.semaphore_signal(barrier, inc=1, device_id=(other,), device_id_type=MESH)
    peers = jnp.int32(4)
    for link in ("up", "down"):

        @pl.when(present[link])
        def _(link=link):
            pl.semaphore_signal(barrier, inc=1, device_id=(device[link],), device_id_type=MESH)

        peers = peers + present[link].astype(jnp.int32)

    windows = (win_bases, win_shift)

    def exists(delta):
        return (chip + delta >= 0) & (chip + delta < total)

    def slot_of(delta, holder):
        return 2 * (PLANE + delta) + holder

    def block_of(kind, delta, holder, leaf):
        block = windows[kind].at[slot_of(delta, holder)]
        return block if leaf is None else block.at[leaf]

    def hop(kind, at, link, order):
        item = OUTBOUND[kind][at][link][order]
        delta, leaf = shift_of(at, item), item[2]
        moved = {"x": at - (at ^ 1), "y": at - (at ^ 2), "up": -PLANE, "down": PLANE}[link]
        return pltpu.make_async_remote_copy(
            src_ref=block_of(kind, delta, core, leaf),
            dst_ref=block_of(kind, delta + moved, core, leaf),
            send_sem=send.at[kind, LINKS.index(link), order],
            recv_sem=recv.at[kind, PLANE + delta + moved, leaf or 0],
            device_id=(device[link],),
            device_id_type=MESH,
        )

    def arrival(kind, delta, leaf):
        there = block_of(kind, delta, core, leaf)
        return pltpu.make_async_remote_copy(
            src_ref=there,
            dst_ref=there,
            send_sem=send.at[kind, 0, 0],
            recv_sem=recv.at[kind, PLANE + delta, leaf or 0],
            device_id=(sibling,),
            device_id_type=MESH,
        )

    def relay(kind, delta, leaf):
        there = block_of(kind, delta, core, leaf)
        return pltpu.make_async_remote_copy(
            src_ref=there,
            dst_ref=there,
            send_sem=pass_send.at[kind, PLANE + delta, leaf or 0],
            recv_sem=pass_recv.at[kind, PLANE + delta, leaf or 0],
            device_id=(sibling,),
            device_id_type=MESH,
        )

    def relayed(kind, delta, leaf):
        there = block_of(kind, delta, 1 - core, leaf)
        return pltpu.make_async_remote_copy(
            src_ref=there,
            dst_ref=there,
            send_sem=pass_send.at[kind, PLANE + delta, leaf or 0],
            recv_sem=pass_recv.at[kind, PLANE + delta, leaf or 0],
            device_id=(sibling,),
            device_id_type=MESH,
        )

    def parts(kind):
        return (None,) if kind else range(per_device)

    def on_links(kind, at, item, act):
        for link in LINKS:
            for order, entry in enumerate(OUTBOUND[kind][at][link]):
                if entry == item:
                    if link in present:
                        pl.when(present[link])(lambda: act(hop(kind, at, link, order)))
                    else:
                        act(hop(kind, at, link, order))

    def start(copy):
        copy.start()

    def stop(copy):
        copy.wait_send()

    def by_place(act):
        for at in range(PLANE):
            pl.when(place == at)(lambda: act(at))

    def dispatch(kind, leaf):
        by_place(lambda at: on_links(kind, at, (0, at, leaf), start))
        relay(kind, 0, leaf).start()

    def serve(kind, step):
        def act(at):
            for now, item in ARRIVALS[kind][at]:
                if now == step:
                    delta, leaf = shift_of(at, item), item[2]

                    def one():
                        arrival(kind, delta, leaf).wait_recv()
                        on_links(kind, at, item, start)
                        relay(kind, delta, leaf).start()

                    if item[0] == 0:
                        one()
                    else:
                        pl.when(exists(delta))(one)

        by_place(act)

    def finish(kind):
        def act(at):
            for leaf in parts(kind):
                on_links(kind, at, (0, at, leaf), stop)
            for _, item in ARRIVALS[kind][at]:
                delta, leaf = shift_of(at, item), item[2]

                def one():
                    on_links(kind, at, item, stop)
                    relay(kind, delta, leaf).wait_send()

                if item[0] == 0:
                    one()
                else:
                    pl.when(exists(delta))(one)

        by_place(act)
        for leaf in parts(kind):
            relay(kind, 0, leaf).wait_send()

    number = me * per_device
    parent = number // CHILDREN
    low = jnp.clip(parent - targets // 2, 0, parents - targets)
    home = parent - low
    inputs[1].wait()
    pl.semaphore_wait(barrier, peers)
    dispatch(0, 0)
    inputs[2].wait()
    reduce_blocks(diag_in, win_bases.at[here], bases_t, work, low_corner)

    def clear():
        blocks[...] = jnp.zeros_like(blocks)
        halves[:, slots] = jnp.zeros_like(halves[:, slots])

    reach = found.shape[1]
    table = pltpu.make_async_copy(found, lookup, found_sem)

    def look_up():
        offset = lax.broadcasted_iota(jnp.int32, (reach, slots), 0) - reach // 2
        order = lax.broadcasted_iota(jnp.int32, (reach, slots), 1)
        inputs[0].wait()
        for leaf in range(per_device):
            away = offset + number + leaf
            hit = (nbrs_in[leaf : leaf + 1, :] == away) & (away >= 0)
            slot = jnp.max(jnp.where(hit, order, -1), axis=1, keepdims=True)
            found[leaf] = jnp.broadcast_to(jnp.where(slot < 0, slots, slot), found.shape[1:])
        table.start()

    unroll = max(n for n in range(1, 14) if slots % n == 0)

    def project(turn):
        for k in range(unroll):
            n = turn * unroll + k
            for leaf in range(per_device):
                halves[leaf, n] = matmul(bases_t[leaf], near_in[leaf, n]).astype(jnp.bfloat16)

    orders = [chunk_order(at) for at in range(PLANE)]
    chunks = len(orders[0][0])

    def pick(values):
        chosen = jnp.int32(values[0])
        for at in range(1, PLANE):
            chosen = jnp.where(place == at, jnp.int32(values[at]), chosen)
        return chosen

    deltas = [pick([order[0][turn] for order in orders]) for turn in range(chunks)]

    def pairs_of(turn):
        delta = deltas[turn]
        for holder in range(2):
            for leaf in range(per_device):
                other = ((chip + delta) * 2 + holder) * per_device + leaf
                column = pl.multiple_of((other % CHILDREN) * RANK, RANK)
                yield holder, leaf, slot_of(delta, holder), other, other // CHILDREN - low, column

    def keep(turn, values):
        for (other, row, column, mine), act in values:
            if turn in (3, 4):
                apart = other - number - mine
                pl.when((apart <= REACH) & (apart >= -REACH))(lambda: act(row, column, mine))
            else:
                act(row, column, mine)

    def first_half(turn):
        for leaf in parts(0):
            relayed(0, deltas[turn], leaf).wait_recv()
        coupled = {}
        targets_of = {}
        for holder, leaf, slot, other, row, column in pairs_of(turn):
            left = []
            for mine in range(per_device):
                n = lookup[mine, other - number - mine + reach // 2, 0]
                left.append(halves[mine, n])
                targets_of[holder, leaf, mine] = (other, row, column, mine)
            both = matmul(jnp.concatenate(left, axis=0), win_bases[slot, leaf])
            for mine in range(per_device):
                part = both[mine * 2 * RANK : (mine + 1) * 2 * RANK]
                high, low_part = split(part[red:, :red])
                here_rows = pl.ds(mine * RANK, RANK)
                lefts[turn, holder, leaf, here_rows, :red] = high
                lefts[turn, holder, leaf, here_rows, red:] = low_part
                coupled[holder, leaf, mine] = (split(part[:red, red:]), part[red:, red:])
        kept = []
        for holder in range(2):
            for mine in range(per_device):
                tall = [
                    jnp.concatenate(coupled[holder, leaf, mine][0], axis=0)
                    for leaf in range(per_device)
                ]
                moved = matmul(turned[mine], jnp.concatenate(tall, axis=1))
                for leaf in range(per_device):
                    value = coupled[holder, leaf, mine][1] + moved[:, leaf * RANK : (leaf + 1) * RANK]

                    def act(row, column, mine, value=value):
                        blocks[mine, row, :, pl.ds(column, RANK)] = value

                    kept.append((targets_of[holder, leaf, mine], act))
        keep(turn, kept)

    def second_half(turn):
        for leaf in parts(1):
            relayed(1, deltas[turn], leaf).wait_recv()
        kept = []
        for holder, leaf, slot, other, row, column in pairs_of(turn):
            moved = win_shift[slot, leaf]
            both = matmul(lefts[turn, holder, leaf], jnp.concatenate([moved, moved], axis=0))
            for mine in range(per_device):
                value = both[mine * RANK : (mine + 1) * RANK]

                def act(row, column, mine, value=value):
                    spot = blocks[mine, row, :, pl.ds(column, RANK)]
                    blocks[mine, row, :, pl.ds(column, RANK)] = spot - value

                kept.append(((other, row, column, mine), act))
        keep(turn, kept)

    def run(half, turn):
        pl.when(exists(deltas[turn]))(lambda: half(turn))

    def row_copy(t):
        other = (seat + t) % size
        width = per_device * RANK
        return pltpu.make_async_remote_copy(
            src_ref=diagonal.at[:, :, pl.ds(pl.multiple_of(other * width, 128), width)],
            dst_ref=landed.at[size - t],
            send_sem=row_send.at[t],
            recv_sem=row_recv.at[size - t],
            device_id=(me - seat + other,),
            device_id_type=MESH,
        )

    def send_rows():
        for leaf in range(per_device):
            column = pl.multiple_of(((number + leaf) % CHILDREN) * RANK, RANK)
            blocks[leaf, home, :, pl.ds(column, RANK)] = skeleton[leaf]
        for leaf in range(per_device):
            diagonal[leaf] = blocks[leaf, home].astype(jnp.bfloat16)
        for t in range(1, size):
            row_copy(t).start()

    def wait_near():
        for copy in fetches:
            copy.wait()
        table.wait()

    def between(panel_done):
        pass
        if panel_done == 0:
            dispatch(0, 1)
        if panel_done == 2:
            serve(0, 1)

    eliminate(win_shift.at[here], turned, work, rows, between)
    dispatch(1, None)
    finish_factor(factor, panel, skeleton, rows, low_corner)
    clear()
    look_up()
    wait_near()
    serve(0, 2)
    project(0)
    project(1)
    run(first_half, 0)
    run(first_half, 1)
    serve(1, 1)
    serve(0, 3)
    run(second_half, 0)
    run(second_half, 1)
    run(first_half, 2)
    run(first_half, 3)
    run(first_half, 4)
    send_rows()
    serve(1, 2)
    run(second_half, 2)
    run(second_half, 3)
    run(second_half, 4)
    serve(0, 4)
    run(first_half, 5)
    run(first_half, 6)
    serve(1, 3)
    run(second_half, 5)
    run(second_half, 6)
    serve(0, 5)
    run(first_half, 7)
    run(first_half, 8)
    run(second_half, 7)
    run(second_half, 8)
    finish(0)
    finish(1)
    for t in range(1, size):
        row_copy(size - t).wait_recv()
    for t in range(1, size):
        row_copy(t).wait_send()


def place_kernel(
    parents, factor, panel, blocks, landed, factor_out, panel_out, merged, block_out, block, sems
):
    per_device, targets = blocks.shape[0], blocks.shape[1]
    size = landed.shape[0]
    width = per_device * RANK
    me = lax.axis_index("leaf")
    seat = me % size
    parent = me * per_device // CHILDREN
    low = jnp.clip(parent - targets // 2, 0, parents.shape[0] - targets)
    copies = []

    def put(source, target):
        copy = pltpu.make_async_copy(source, target, sems.at[len(copies)])
        copy.start()
        copies.append(copy)

    for q in range(targets):
        row = parents[parent, q] - low
        for leaf in range(per_device):
            put(blocks.at[leaf, row], merged.at[leaf, q])
    put(factor, factor_out)
    put(panel, panel_out)
    for t in range(size):
        columns = pl.ds(pl.multiple_of(((seat + t) % size) * width, 128), width)
        mine = blocks[:, parent - low, :, columns].reshape(width, width)
        if t == 0:
            theirs = mine
        else:
            theirs = landed[t].reshape(width, width).astype(jnp.float32)
        block[:, columns] = 0.5 * (mine + theirs.T)
        put(block.at[:, columns], block_out.at[:, columns])
    for copy in copies:
        copy.wait()


def local(count, near_blocks, diag_blocks, bases, leaf_nbrs, parent_nbrs):
    per_device, leaf_rows = bases.shape[0], bases.shape[1]
    red = leaf_rows - RANK
    slots = near_blocks.shape[1]
    parents, targets = parent_nbrs.shape
    assert per_device == 2 and REACH == 4 * PLANE
    vmem = pl.BlockSpec(memory_space=pltpu.VMEM)
    smem = pl.BlockSpec(memory_space=pltpu.SMEM)
    hbm = pl.BlockSpec(memory_space=pltpu.HBM)
    f32, bf16 = jnp.float32, jnp.bfloat16

    def in_hbm(array):
        return pltpu.with_memory_space_constraint(array, pltpu.HBM)

    def out(shape, dtype):
        return jax.ShapeDtypeStruct(shape, dtype)

    reach = 2 * (REACH + CHILDREN)
    size = CHILDREN // per_device
    width = per_device * RANK
    window = 2 * (2 * PLANE + 1)
    links = max(len(out_[link]) for kind in OUTBOUND for out_ in kind for link in LINKS)
    sems = pltpu.SemaphoreType.DMA
    factor, panel, blocks, landed = pl.pallas_call(
        functools.partial(level_kernel, count, parents, targets),
        out_shape=(
            out((per_device, red, red), f32),
            out((per_device, red, RANK), f32),
            out((per_device, targets, RANK, CHILDREN * RANK), f32),
            out((size, per_device, RANK, width), bf16),
        ),
        in_specs=[hbm] * 4,
        out_specs=(vmem,) * 4,
        scratch_shapes=[
            pltpu.VMEM((window,) + bases.shape, bf16),
            pltpu.VMEM((window, per_device, red, RANK), bf16),
            pltpu.VMEM(diag_blocks.shape, bf16),
            pltpu.VMEM(leaf_nbrs.shape, jnp.int32),
            pltpu.VMEM((per_device, RANK, RANK), f32),
            pltpu.VMEM((per_device, RANK, RANK), f32),
            pltpu.VMEM((per_device, RANK, 2 * red), bf16),
            pltpu.VMEM(bases.shape, bf16),
            pltpu.VMEM((per_device, red, 2 * red + RANK), f32),
            pltpu.VMEM((per_device, red, 2 * red + RANK), f32),
            pltpu.VMEM(near_blocks.shape, bf16),
            pltpu.VMEM((per_device, slots + 1) + near_blocks.shape[2:], bf16),
            pltpu.VMEM((2 * PLANE + 1, 2, per_device, per_device * RANK, 2 * red), bf16),
            pltpu.VMEM((per_device, RANK, CHILDREN * RANK), bf16),
            sems((2, len(LINKS), links)),
            sems((2, 2 * PLANE + 1, per_device)),
            sems((2, 2 * PLANE + 1, per_device)),
            sems((2, 2 * PLANE + 1, per_device)),
            sems((3,)),
            sems((per_device,)),
            sems((size,)),
            sems((size,)),
            pltpu.VMEM((per_device, reach, 128), jnp.int32),
            pltpu.SMEM((per_device, reach, 128), jnp.int32),
            sems(()),
        ],
        compiler_params=pltpu.CompilerParams(
            collective_id=0, has_side_effects=True, vmem_limit_bytes=46_500_000
        ),
        name="level",
    )(*(in_hbm(array) for array in (leaf_nbrs, diag_blocks, bases, near_blocks)))

    return pl.pallas_call(
        place_kernel,
        out_shape=(
            out((per_device, red, red), f32),
            out((per_device, red, RANK), f32),
            out((per_device, targets, RANK, CHILDREN * RANK), f32),
            out((width, CHILDREN * RANK), f32),
        ),
        in_specs=[smem, vmem, vmem, vmem, vmem],
        out_specs=(hbm,) * 4,
        scratch_shapes=[
            pltpu.VMEM((width, CHILDREN * RANK), f32),
            sems((targets * per_device + 2 + size,)),
        ],
        compiler_params=pltpu.CompilerParams(vmem_limit_bytes=16_000_000),
        name="place",
    )(parent_nbrs, factor, panel, blocks, landed)


def solution(mesh):
    count = mesh.shape["leaf"]
    in_specs = (
        P("leaf", None, None, None),
        P("leaf", None, None),
        P("leaf", None, None),
        P("leaf", None),
        P(),
    )
    out_specs = (
        P("leaf", None, None),
        P("leaf", None, None),
        P("leaf", None, None, None),
        P("leaf", None),
    )
    return jax.shard_map(
        functools.partial(local, count),
        mesh=mesh,
        in_specs=in_specs,
        out_specs=out_specs,
        check_vma=False,
    )
```

```python
import functools

import jax
import jax.numpy as jnp
from jax import lax
from jax.experimental import pallas as pl
from jax.experimental.pallas import tpu as pltpu
from jax.sharding import PartitionSpec as P

RANK = 128
REACH = 16
CHILDREN = 8
PANEL = 32
GROUP = 8
LANES = 128
PLANE = 4
LINKS = ("x", "y", "up", "down")
MESH = pl.DeviceIdType.MESH
highest = lax.Precision.HIGHEST


def matmul(a, b):
    return jnp.dot(a, b, preferred_element_type=jnp.float32)


def matmul_t(a, b, precision=None):
    return lax.dot_general(
        a, b, (((0,), (0,)), ((), ())), preferred_element_type=jnp.float32, precision=precision
    )


def halves_of(plane, chip):
    return [(plane, chip, 0), (plane, chip, 1)]


def whole(plane, chip):
    return [(plane, chip, None)]


OUTER_IN = (
    {
        "x": halves_of(0, 1) + [(0, 3, 0), (-1, 1, 0)],
        "y": halves_of(0, 2) + [(0, 3, 1)] + halves_of(-1, 2),
        "up": halves_of(-1, 0) + [(-1, 1, 1)] + halves_of(-1, 3),
        "down": halves_of(1, 0),
    },
    {
        "x": halves_of(0, 0) + [(0, 2, 0)],
        "y": halves_of(0, 3) + [(0, 2, 1), (-1, 3, 0)],
        "up": halves_of(-1, 1) + [(-1, 3, 1)] + halves_of(-1, 2),
        "down": halves_of(1, 1) + halves_of(1, 0),
    },
    {
        "x": halves_of(0, 3) + [(0, 1, 0)],
        "y": halves_of(0, 0) + [(0, 1, 1), (1, 0, 0)],
        "up": halves_of(-1, 2) + halves_of(-1, 3),
        "down": halves_of(1, 2) + [(1, 0, 1)] + halves_of(1, 1),
    },
    {
        "x": halves_of(0, 2) + [(0, 0, 0), (1, 2, 0)],
        "y": halves_of(0, 1) + [(0, 0, 1)] + halves_of(1, 1),
        "up": halves_of(-1, 3),
        "down": halves_of(1, 3) + [(1, 2, 1)] + halves_of(1, 0),
    },
)
LIFTED_IN = (
    {
        "x": whole(0, 1) + whole(-1, 1),
        "y": whole(0, 2) + whole(0, 3) + whole(-1, 2),
        "up": whole(-1, 0) + whole(-1, 3),
        "down": whole(1, 0),
    },
    {
        "x": whole(0, 0) + whole(0, 2),
        "y": whole(0, 3) + whole(-1, 3),
        "up": whole(-1, 1) + whole(-1, 2),
        "down": whole(1, 1) + whole(1, 0),
    },
    {
        "x": whole(0, 3) + whole(0, 1),
        "y": whole(0, 0) + whole(1, 0),
        "up": whole(-1, 2) + whole(-1, 3),
        "down": whole(1, 2) + whole(1, 1),
    },
    {
        "x": whole(0, 2) + whole(1, 2),
        "y": whole(0, 1) + whole(0, 0) + whole(1, 1),
        "up": whole(-1, 3),
        "down": whole(1, 3) + whole(1, 0),
    },
)


def plan(inbound):
    outbound = []
    for place in range(PLANE):
        out = {"x": inbound[place ^ 1]["x"], "y": inbound[place ^ 2]["y"]}
        out["up"] = [(plane + 1, chip, leaf) for plane, chip, leaf in inbound[place]["up"]]
        out["down"] = [(plane - 1, chip, leaf) for plane, chip, leaf in inbound[place]["down"]]
        outbound.append(out)
    held = [{(0, place, leaf): 0 for leaf in (0, 1, None)} for place in range(PLANE)]
    arrivals = [[] for _ in range(PLANE)]
    queue = {(place, link): 0 for place in range(PLANE) for link in LINKS}
    now = 0
    while any(queue[place, link] < len(outbound[place][link]) for place, link in queue):
        now += 1
        landed = []
        for (place, link), done in queue.items():
            items = outbound[place][link]
            if done < len(items) and held[place].get(items[done], now) < now:
                target = {"x": place ^ 1, "y": place ^ 2}.get(link, place)
                landed.append((target, inbound[target][link][done]))
                queue[place, link] = done + 1
        for target, item in landed:
            held[target][item] = now
            arrivals[target].append((now, item))
    return outbound, arrivals, now


OUTBOUND, ARRIVALS, STEPS = zip(plan(OUTER_IN), plan(LIFTED_IN))


def shift_of(place, item):
    plane, chip, _ = item
    return PLANE * plane + chip - place


def chunk_order(place):
    ready = [{0: 0}, {0: 0}]
    for kind in range(2):
        for now, item in ARRIVALS[kind][place]:
            ready[kind][shift_of(place, item)] = now
    first = [0, (place ^ 1) - place, (place ^ 2) - place, -PLANE, PLANE]
    rest = sorted((ready[1][delta], now, delta) for delta, now in ready[0].items() if delta not in first)
    order = first + [delta for _, _, delta in rest]
    return order, [(ready[0][delta], ready[1][delta]) for delta in order]


def reduce_blocks(diag, bases, bases_t, work, low_corner):
    per_device, leaf_rows = bases.shape[0], bases.shape[1]
    red = leaf_rows - RANK
    row_id = lax.broadcasted_iota(jnp.int32, (red, red), 0)
    col_id = lax.broadcasted_iota(jnp.int32, (red, red), 1)
    for leaf in range(per_device):
        basis = bases[leaf]
        basis_t = basis.T
        bases_t[leaf] = basis_t
        half = matmul(basis_t, diag[leaf]).astype(jnp.bfloat16)
        dense = matmul(half, basis)
        top = dense[:red, :red]
        work[leaf, :, :red] = 0.5 * (top + top.T)
        work[leaf, :, red : red + RANK] = dense[:red, red:]
        work[leaf, :, red + RANK :] = (row_id == col_id).astype(jnp.float32)
        low_corner[leaf] = dense[red:, red:]


def eliminate(bases, lifted, turned, work, rows, serve):
    per_device, red = work.shape[0], work.shape[1]
    tiles = work.shape[2] // LANES
    row_id = lax.broadcasted_iota(jnp.int32, (red, red), 0)
    col_id = lax.broadcasted_iota(jnp.int32, (red, red), 1)
    sub = lax.broadcasted_iota(jnp.int32, (GROUP, LANES), 0)
    groups = PANEL // GROUP
    leaves = range(per_device)
    for start in range(0, red, PANEL):
        strips = [
            [
                [
                    work[leaf, pl.ds(start + GROUP * v, GROUP), pl.ds(LANES * t, LANES)]
                    for t in range(tiles)
                ]
                for v in range(groups)
            ]
            for leaf in leaves
        ]
        for g in range(groups):
            first = start + GROUP * g
            columns = [
                {
                    v: [
                        jnp.broadcast_to(strips[leaf][v][0][:, first + c : first + c + 1], (GROUP, LANES))
                        for c in range(GROUP)
                    ]
                    for v in range(g, groups)
                }
                for leaf in leaves
            ]
            for r in range(GROUP):
                for leaf in leaves:
                    cols, strip = columns[leaf], strips[leaf]
                    inverse = 1.0 / cols[g][r][r : r + 1]
                    heads = [cols[g][c][r : r + 1] for c in range(GROUP)]
                    lines = [strip[g][t][r : r + 1] for t in range(tiles)]
                    for v in range(g, groups):
                        ratio = cols[v][r] * inverse
                        if v == g:
                            ratio = jnp.where(sub > r, ratio, 0.0)
                        for c in range(r + 1, GROUP):
                            cols[v][c] = cols[v][c] - ratio * heads[c]
                        for t in range(tiles):
                            strip[v][t] = strip[v][t] - ratio * lines[t]
            for leaf in leaves:
                pivots = columns[leaf][g][0]
                for r in range(1, GROUP):
                    pivots = jnp.where(sub == r, columns[leaf][g][r], pivots)
                scale = 1.0 / jnp.sqrt(pivots)
                for t in range(tiles):
                    here = (leaf, pl.ds(first, GROUP), pl.ds(LANES * t, LANES))
                    rows[here] = strips[leaf][g][t] * scale
        if start + PANEL < red:
            for leaf in leaves:
                strip = rows[leaf, start : start + PANEL, :]
                work[leaf] = work[leaf] - matmul_t(strip[:, :red], strip, highest)
        serve(start // PANEL)
    for leaf in range(per_device):
        solved = rows[leaf, :, red : red + RANK]
        inverse = jnp.where(col_id <= row_id, rows[leaf, :, red + RANK :], 0.0)
        shift = matmul_t(inverse, solved, highest).astype(jnp.bfloat16)
        lifted[leaf] = matmul(bases[leaf, :, :red], shift).astype(jnp.bfloat16)
        back = -shift.astype(jnp.float32).T
        turned[leaf, :, :red] = back.astype(jnp.bfloat16)
        turned[leaf, :, red:] = back.astype(jnp.bfloat16)


def finish_factor(factor, panel, skeleton, rows, low_corner):
    per_device, red = rows.shape[0], rows.shape[1]
    row_id = lax.broadcasted_iota(jnp.int32, (red, red), 0)
    col_id = lax.broadcasted_iota(jnp.int32, (red, red), 1)
    for leaf in range(per_device):
        solved = rows[leaf, :, red : red + RANK]
        panel[leaf] = solved
        skeleton[leaf] = low_corner[leaf] - matmul_t(solved, solved, highest)
        upper = jnp.where(col_id >= row_id, rows[leaf, :, :red], 0.0)
        factor[leaf] = upper.T


def split(values):
    high = values.astype(jnp.bfloat16)
    return high, (values - high.astype(jnp.float32)).astype(jnp.bfloat16)


def level_kernel(
    count,
    parents,
    targets,
    nbrs,
    diag,
    bases,
    near,
    factor,
    panel,
    blocks,
    landed,
    win_outer,
    win_lifted,
    bases_in,
    diag_in,
    nbrs_in,
    low_corner,
    skeleton,
    turned,
    bases_t,
    work,
    rows,
    near_in,
    halves,
    diagonal,
    send,
    recv,
    pass_send,
    pass_recv,
    in_sem,
    near_sem,
    row_send,
    row_recv,
    found,
    lookup,
    found_sem,
):
    per_device, slots = near_in.shape[0], near_in.shape[1]
    red = rows.shape[1]
    total = count // 2
    me = lax.axis_index("leaf")
    core, chip = me % 2, me // 2
    sibling = me + 1 - 2 * core
    place = chip % PLANE
    size = CHILDREN // per_device
    seat = me % size
    across = me + 2 * (1 - 2 * (place % 2))
    along = me + 4 * (1 - 2 * (place // 2))
    device = {"x": across, "y": along, "up": me + 2 * PLANE, "down": me - 2 * PLANE}
    present = {"up": chip + PLANE < total, "down": chip - PLANE >= 0}
    far = across + 1 - 2 * core

    fetches = [
        pltpu.make_async_copy(near.at[leaf], near_in.at[leaf], near_sem.at[leaf])
        for leaf in range(per_device)
    ]
    here = 2 * PLANE + core
    inputs = [
        pltpu.make_async_copy(source, target, in_sem.at[n])
        for n, (source, target) in enumerate(
            (
                (nbrs, nbrs_in),
                (bases.at[:, :, pl.ds(red, RANK)], win_outer.at[here]),
                (bases, bases_in),
                (diag, diag_in),
            )
        )
    ]
    for copy in inputs + fetches:
        copy.start()

    barrier = pltpu.get_barrier_semaphore()
    for other in (sibling, across, along, far):
        pl.semaphore_signal(barrier, inc=1, device_id=(other,), device_id_type=MESH)
    peers = jnp.int32(4)
    for link in ("up", "down"):

        @pl.when(present[link])
        def _(link=link):
            pl.semaphore_signal(barrier, inc=1, device_id=(device[link],), device_id_type=MESH)

        peers = peers + present[link].astype(jnp.int32)

    windows = (win_outer, win_lifted)

    def exists(delta):
        return (chip + delta >= 0) & (chip + delta < total)

    def slot_of(delta, holder):
        return 2 * (PLANE + delta) + holder

    def block_of(kind, delta, holder, leaf):
        block = windows[kind].at[slot_of(delta, holder)]
        return block if leaf is None else block.at[leaf]

    def hop(kind, at, link, order):
        item = OUTBOUND[kind][at][link][order]
        delta, leaf = shift_of(at, item), item[2]
        moved = {"x": at - (at ^ 1), "y": at - (at ^ 2), "up": -PLANE, "down": PLANE}[link]
        return pltpu.make_async_remote_copy(
            src_ref=block_of(kind, delta, core, leaf),
            dst_ref=block_of(kind, delta + moved, core, leaf),
            send_sem=send.at[kind, LINKS.index(link), order],
            recv_sem=recv.at[kind, PLANE + delta + moved, leaf or 0],
            device_id=(device[link],),
            device_id_type=MESH,
        )

    def arrival(kind, delta, leaf):
        there = block_of(kind, delta, core, leaf)
        return pltpu.make_async_remote_copy(
            src_ref=there,
            dst_ref=there,
            send_sem=send.at[kind, 0, 0],
            recv_sem=recv.at[kind, PLANE + delta, leaf or 0],
            device_id=(sibling,),
            device_id_type=MESH,
        )

    def relay(kind, delta, leaf):
        there = block_of(kind, delta, core, leaf)
        return pltpu.make_async_remote_copy(
            src_ref=there,
            dst_ref=there,
            send_sem=pass_send.at[kind, PLANE + delta, leaf or 0],
            recv_sem=pass_recv.at[kind, PLANE + delta, leaf or 0],
            device_id=(sibling,),
            device_id_type=MESH,
        )

    def relayed(kind, delta, leaf):
        there = block_of(kind, delta, 1 - core, leaf)
        return pltpu.make_async_remote_copy(
            src_ref=there,
            dst_ref=there,
            send_sem=pass_send.at[kind, PLANE + delta, leaf or 0],
            recv_sem=pass_recv.at[kind, PLANE + delta, leaf or 0],
            device_id=(sibling,),
            device_id_type=MESH,
        )

    def parts(kind):
        return (None,) if kind else range(per_device)

    def on_links(kind, at, item, act):
        for link in LINKS:
            for order, entry in enumerate(OUTBOUND[kind][at][link]):
                if entry == item:
                    if link in present:
                        pl.when(present[link])(lambda: act(hop(kind, at, link, order)))
                    else:
                        act(hop(kind, at, link, order))

    def start(copy):
        copy.start()

    def stop(copy):
        copy.wait_send()

    def by_place(act):
        for at in range(PLANE):
            pl.when(place == at)(lambda: act(at))

    def dispatch(kind, leaf):
        by_place(lambda at: on_links(kind, at, (0, at, leaf), start))
        relay(kind, 0, leaf).start()

    def serve(kind, step):
        def act(at):
            for now, item in ARRIVALS[kind][at]:
                if now == step:
                    delta, leaf = shift_of(at, item), item[2]

                    def one():
                        arrival(kind, delta, leaf).wait_recv()
                        on_links(kind, at, item, start)
                        relay(kind, delta, leaf).start()

                    if item[0] == 0:
                        one()
                    else:
                        pl.when(exists(delta))(one)

        by_place(act)

    def finish(kind):
        def act(at):
            for leaf in parts(kind):
                on_links(kind, at, (0, at, leaf), stop)
            for _, item in ARRIVALS[kind][at]:
                delta, leaf = shift_of(at, item), item[2]

                def one():
                    on_links(kind, at, item, stop)
                    relay(kind, delta, leaf).wait_send()

                if item[0] == 0:
                    one()
                else:
                    pl.when(exists(delta))(one)

        by_place(act)
        for leaf in parts(kind):
            relay(kind, 0, leaf).wait_send()

    number = me * per_device
    parent = number // CHILDREN
    low = jnp.clip(parent - targets // 2, 0, parents - targets)
    home = parent - low
    inputs[1].wait()
    pl.semaphore_wait(barrier, peers)
    dispatch(0, 0)
    for copy in inputs[2:]:
        copy.wait()
    reduce_blocks(diag_in, bases_in, bases_t, work, low_corner)

    def clear():
        for row in range(targets):

            @pl.when((low + row < parent - 1) | (low + row > parent + 1))
            def _(row=row):
                blocks[:, row] = jnp.zeros_like(blocks[:, row])

        halves[:, slots] = jnp.zeros_like(halves[:, slots])

    reach = found.shape[1]
    table = pltpu.make_async_copy(found, lookup, found_sem)

    def look_up():
        offset = lax.broadcasted_iota(jnp.int32, (reach, slots), 0) - reach // 2
        order = lax.broadcasted_iota(jnp.int32, (reach, slots), 1)
        inputs[0].wait()
        for leaf in range(per_device):
            away = offset + number + leaf
            hit = (nbrs_in[leaf : leaf + 1, :] == away) & (away >= 0)
            slot = jnp.max(jnp.where(hit, order, -1), axis=1, keepdims=True)
            found[leaf] = jnp.broadcast_to(jnp.where(slot < 0, slots, slot), found.shape[1:])
        table.start()

    unroll = max(n for n in range(1, 14) if slots % n == 0)

    def project(turn):
        for k in range(unroll):
            n = turn * unroll + k
            for leaf in range(per_device):
                halves[leaf, n] = matmul(bases_t[leaf], near_in[leaf, n]).astype(jnp.bfloat16)

    orders = [chunk_order(at) for at in range(PLANE)]
    chunks = len(orders[0][0])

    def pick(values):
        chosen = jnp.int32(values[0])
        for at in range(1, PLANE):
            chosen = jnp.where(place == at, jnp.int32(values[at]), chosen)
        return chosen

    deltas = [pick([order[0][turn] for order in orders]) for turn in range(chunks)]

    def pairs_of(turn):
        delta = deltas[turn]
        for holder in range(2):
            for leaf in range(per_device):
                other = ((chip + delta) * 2 + holder) * per_device + leaf
                column = pl.multiple_of((other % CHILDREN) * RANK, RANK)
                yield holder, leaf, slot_of(delta, holder), other, other // CHILDREN - low, column

    def keep(turn, values):
        for (other, row, column, mine), act in values:
            if turn in (3, 4):
                apart = other - number - mine
                pl.when((apart <= REACH) & (apart >= -REACH))(lambda: act(row, column, mine))
            else:
                act(row, column, mine)

    def slot_for(other, mine):
        return lookup[mine, other - number - mine + reach // 2, 0]

    def first_half(turn):
        for leaf in parts(0):
            relayed(0, deltas[turn], leaf).wait_recv()
        coupled = {}
        targets_of = {}
        for holder, leaf, slot, other, row, column in pairs_of(turn):
            left = [halves[mine, slot_for(other, mine)] for mine in range(per_device)]
            both = matmul(jnp.concatenate(left, axis=0), win_outer[slot, leaf])
            for mine in range(per_device):
                targets_of[holder, leaf, mine] = (other, row, column, mine)
                part = both[mine * 2 * RANK : (mine + 1) * 2 * RANK]
                coupled[holder, leaf, mine] = (split(part[:red]), part[red:])
        kept = []
        for holder in range(2):
            for mine in range(per_device):
                tall = [
                    jnp.concatenate(coupled[holder, leaf, mine][0], axis=0)
                    for leaf in range(per_device)
                ]
                moved = matmul(turned[mine], jnp.concatenate(tall, axis=1))
                for leaf in range(per_device):
                    value = coupled[holder, leaf, mine][1] + moved[:, leaf * RANK : (leaf + 1) * RANK]

                    def act(row, column, mine, value=value):
                        blocks[mine, row, :, pl.ds(column, RANK)] = value

                    kept.append((targets_of[holder, leaf, mine], act))
        keep(turn, kept)

    def second_half(turn):
        for leaf in parts(1):
            relayed(1, deltas[turn], leaf).wait_recv()
        kept = []
        for holder, leaf, slot, other, row, column in pairs_of(turn):
            left = [halves[mine, slot_for(other, mine), red:] for mine in range(per_device)]
            both = matmul(jnp.concatenate(left, axis=0), win_lifted[slot, leaf])
            for mine in range(per_device):
                value = both[mine * RANK : (mine + 1) * RANK]

                def act(row, column, mine, value=value):
                    spot = blocks[mine, row, :, pl.ds(column, RANK)]
                    blocks[mine, row, :, pl.ds(column, RANK)] = spot - value

                kept.append(((other, row, column, mine), act))
        keep(turn, kept)

    def run(half, turn):
        pl.when(exists(deltas[turn]))(lambda: half(turn))

    def row_copy(t):
        other = (seat + t) % size
        width = per_device * RANK
        return pltpu.make_async_remote_copy(
            src_ref=diagonal.at[:, :, pl.ds(pl.multiple_of(other * width, 128), width)],
            dst_ref=landed.at[size - t],
            send_sem=row_send.at[t],
            recv_sem=row_recv.at[size - t],
            device_id=(me - seat + other,),
            device_id_type=MESH,
        )

    def send_rows():
        for leaf in range(per_device):
            column = pl.multiple_of(((number + leaf) % CHILDREN) * RANK, RANK)
            blocks[leaf, home, :, pl.ds(column, RANK)] = skeleton[leaf]
        for leaf in range(per_device):
            diagonal[leaf] = blocks[leaf, home].astype(jnp.bfloat16)
        for t in range(1, size):
            row_copy(t).start()

    def wait_near():
        for copy in fetches:
            copy.wait()
        table.wait()

    def between(panel_done):
        pass
        if panel_done == 0:
            dispatch(0, 1)
        if panel_done == 2:
            serve(0, 1)

    eliminate(bases_in, win_lifted.at[here], turned, work, rows, between)
    dispatch(1, None)
    finish_factor(factor, panel, skeleton, rows, low_corner)
    clear()
    look_up()
    wait_near()
    serve(0, 2)
    project(0)
    project(1)
    run(first_half, 0)
    run(first_half, 1)
    serve(1, 1)
    serve(0, 3)
    run(second_half, 0)
    run(second_half, 1)
    run(first_half, 2)
    run(first_half, 3)
    run(first_half, 4)
    send_rows()
    serve(0, 4)
    serve(1, 2)
    run(second_half, 2)
    run(second_half, 3)
    run(second_half, 4)
    run(first_half, 5)
    run(first_half, 6)
    serve(0, 5)
    run(first_half, 7)
    run(first_half, 8)
    serve(1, 3)
    run(second_half, 5)
    run(second_half, 6)
    run(second_half, 7)
    run(second_half, 8)
    finish(0)
    finish(1)
    for t in range(1, size):
        row_copy(size - t).wait_recv()
    for t in range(1, size):
        row_copy(t).wait_send()


def place_kernel(
    parents, factor, panel, blocks, landed, factor_out, panel_out, merged, block_out, block, sems
):
    per_device, targets = blocks.shape[0], blocks.shape[1]
    size = landed.shape[0]
    width = per_device * RANK
    me = lax.axis_index("leaf")
    seat = me % size
    parent = me * per_device // CHILDREN
    low = jnp.clip(parent - targets // 2, 0, parents.shape[0] - targets)
    copies = []

    def put(source, target):
        copy = pltpu.make_async_copy(source, target, sems.at[len(copies)])
        copy.start()
        copies.append(copy)

    for q in range(targets):
        row = parents[parent, q] - low
        for leaf in range(per_device):
            put(blocks.at[leaf, row], merged.at[leaf, q])
    put(factor, factor_out)
    put(panel, panel_out)
    for t in range(size):
        columns = pl.ds(pl.multiple_of(((seat + t) % size) * width, 128), width)
        mine = blocks[:, parent - low, :, columns].reshape(width, width)
        if t == 0:
            theirs = mine
        else:
            theirs = landed[t].reshape(width, width).astype(jnp.float32)
        block[:, columns] = 0.5 * (mine + theirs.T)
        put(block.at[:, columns], block_out.at[:, columns])
    for copy in copies:
        copy.wait()


def local(count, near_blocks, diag_blocks, bases, leaf_nbrs, parent_nbrs):
    per_device, leaf_rows = bases.shape[0], bases.shape[1]
    red = leaf_rows - RANK
    slots = near_blocks.shape[1]
    parents, targets = parent_nbrs.shape
    assert per_device == 2 and REACH == 4 * PLANE
    vmem = pl.BlockSpec(memory_space=pltpu.VMEM)
    smem = pl.BlockSpec(memory_space=pltpu.SMEM)
    hbm = pl.BlockSpec(memory_space=pltpu.HBM)
    f32, bf16 = jnp.float32, jnp.bfloat16

    def in_hbm(array):
        return pltpu.with_memory_space_constraint(array, pltpu.HBM)

    def out(shape, dtype):
        return jax.ShapeDtypeStruct(shape, dtype)

    reach = 2 * (REACH + CHILDREN)
    size = CHILDREN // per_device
    width = per_device * RANK
    window = 2 * (2 * PLANE + 1)
    links = max(len(out_[link]) for kind in OUTBOUND for out_ in kind for link in LINKS)
    sems = pltpu.SemaphoreType.DMA
    factor, panel, blocks, landed = pl.pallas_call(
        functools.partial(level_kernel, count, parents, targets),
        out_shape=(
            out((per_device, red, red), f32),
            out((per_device, red, RANK), f32),
            out((per_device, targets, RANK, CHILDREN * RANK), f32),
            out((size, per_device, RANK, width), bf16),
        ),
        in_specs=[hbm] * 4,
        out_specs=(vmem,) * 4,
        scratch_shapes=[
            pltpu.VMEM((window, per_device, leaf_rows, RANK), bf16),
            pltpu.VMEM((window, per_device, leaf_rows, RANK), bf16),
            pltpu.VMEM(bases.shape, bf16),
            pltpu.VMEM(diag_blocks.shape, bf16),
            pltpu.VMEM(leaf_nbrs.shape, jnp.int32),
            pltpu.VMEM((per_device, RANK, RANK), f32),
            pltpu.VMEM((per_device, RANK, RANK), f32),
            pltpu.VMEM((per_device, RANK, 2 * red), bf16),
            pltpu.VMEM(bases.shape, bf16),
            pltpu.VMEM((per_device, red, 2 * red + RANK), f32),
            pltpu.VMEM((per_device, red, 2 * red + RANK), f32),
            pltpu.VMEM(near_blocks.shape, bf16),
            pltpu.VMEM((per_device, slots + 1) + near_blocks.shape[2:], bf16),
            pltpu.VMEM((per_device, RANK, CHILDREN * RANK), bf16),
            sems((2, len(LINKS), links)),
            sems((2, 2 * PLANE + 1, per_device)),
            sems((2, 2 * PLANE + 1, per_device)),
            sems((2, 2 * PLANE + 1, per_device)),
            sems((4,)),
            sems((per_device,)),
            sems((size,)),
            sems((size,)),
            pltpu.VMEM((per_device, reach, 128), jnp.int32),
            pltpu.SMEM((per_device, reach, 128), jnp.int32),
            sems(()),
        ],
        compiler_params=pltpu.CompilerParams(
            collective_id=0, has_side_effects=True, vmem_limit_bytes=46_500_000
        ),
        name="level",
    )(*(in_hbm(array) for array in (leaf_nbrs, diag_blocks, bases, near_blocks)))

    return pl.pallas_call(
        place_kernel,
        out_shape=(
            out((per_device, red, red), f32),
            out((per_device, red, RANK), f32),
            out((per_device, targets, RANK, CHILDREN * RANK), f32),
            out((width, CHILDREN * RANK), f32),
        ),
        in_specs=[smem, vmem, vmem, vmem, vmem],
        out_specs=(hbm,) * 4,
        scratch_shapes=[
            pltpu.VMEM((width, CHILDREN * RANK), f32),
            sems((targets * per_device + 2 + size,)),
        ],
        compiler_params=pltpu.CompilerParams(vmem_limit_bytes=16_000_000),
        name="place",
    )(parent_nbrs, factor, panel, blocks, landed)


def solution(mesh):
    count = mesh.shape["leaf"]
    in_specs = (
        P("leaf", None, None, None),
        P("leaf", None, None),
        P("leaf", None, None),
        P("leaf", None),
        P(),
    )
    out_specs = (
        P("leaf", None, None),
        P("leaf", None, None),
        P("leaf", None, None, None),
        P("leaf", None),
    )
    return jax.shard_map(
        functools.partial(local, count),
        mesh=mesh,
        in_specs=in_specs,
        out_specs=out_specs,
        check_vma=False,
    )
```

```python
import functools

import jax
import jax.numpy as jnp
from jax import lax
from jax.experimental import pallas as pl
from jax.experimental.pallas import tpu as pltpu
from jax.sharding import PartitionSpec as P

RANK = 128
REACH = 16
CHILDREN = 8
PANEL = 32
GROUP = 8
LANES = 128
PLANE = 4
LINKS = ("x", "y", "up", "down")
MESH = pl.DeviceIdType.MESH
highest = lax.Precision.HIGHEST


def matmul(a, b):
    return jnp.dot(a, b, preferred_element_type=jnp.float32)


def matmul_t(a, b, precision=None):
    return lax.dot_general(
        a, b, (((0,), (0,)), ((), ())), preferred_element_type=jnp.float32, precision=precision
    )


def halves_of(plane, chip):
    return [(plane, chip, 0), (plane, chip, 1)]


def whole(plane, chip):
    return [(plane, chip, None)]


OUTER_IN = (
    {
        "x": halves_of(0, 1) + [(0, 3, 0), (-1, 1, 0)],
        "y": halves_of(0, 2) + [(0, 3, 1)] + halves_of(-1, 2),
        "up": halves_of(-1, 0) + [(-1, 1, 1)] + halves_of(-1, 3),
        "down": halves_of(1, 0),
    },
    {
        "x": halves_of(0, 0) + [(0, 2, 0)],
        "y": halves_of(0, 3) + [(0, 2, 1), (-1, 3, 0)],
        "up": halves_of(-1, 1) + [(-1, 3, 1)] + halves_of(-1, 2),
        "down": halves_of(1, 1) + halves_of(1, 0),
    },
    {
        "x": halves_of(0, 3) + [(0, 1, 0)],
        "y": halves_of(0, 0) + [(0, 1, 1), (1, 0, 0)],
        "up": halves_of(-1, 2) + halves_of(-1, 3),
        "down": halves_of(1, 2) + [(1, 0, 1)] + halves_of(1, 1),
    },
    {
        "x": halves_of(0, 2) + [(0, 0, 0), (1, 2, 0)],
        "y": halves_of(0, 1) + [(0, 0, 1)] + halves_of(1, 1),
        "up": halves_of(-1, 3),
        "down": halves_of(1, 3) + [(1, 2, 1)] + halves_of(1, 0),
    },
)
LIFTED_IN = (
    {
        "x": whole(0, 1) + whole(-1, 1),
        "y": whole(0, 2) + whole(0, 3) + whole(-1, 2),
        "up": whole(-1, 0) + whole(-1, 3),
        "down": whole(1, 0),
    },
    {
        "x": whole(0, 0) + whole(0, 2),
        "y": whole(0, 3) + whole(-1, 3),
        "up": whole(-1, 1) + whole(-1, 2),
        "down": whole(1, 1) + whole(1, 0),
    },
    {
        "x": whole(0, 3) + whole(0, 1),
        "y": whole(0, 0) + whole(1, 0),
        "up": whole(-1, 2) + whole(-1, 3),
        "down": whole(1, 2) + whole(1, 1),
    },
    {
        "x": whole(0, 2) + whole(1, 2),
        "y": whole(0, 1) + whole(0, 0) + whole(1, 1),
        "up": whole(-1, 3),
        "down": whole(1, 3) + whole(1, 0),
    },
)


def plan(inbound):
    outbound = []
    for place in range(PLANE):
        out = {"x": inbound[place ^ 1]["x"], "y": inbound[place ^ 2]["y"]}
        out["up"] = [(plane + 1, chip, leaf) for plane, chip, leaf in inbound[place]["up"]]
        out["down"] = [(plane - 1, chip, leaf) for plane, chip, leaf in inbound[place]["down"]]
        outbound.append(out)
    held = [{(0, place, leaf): 0 for leaf in (0, 1, None)} for place in range(PLANE)]
    arrivals = [[] for _ in range(PLANE)]
    queue = {(place, link): 0 for place in range(PLANE) for link in LINKS}
    now = 0
    while any(queue[place, link] < len(outbound[place][link]) for place, link in queue):
        now += 1
        landed = []
        for (place, link), done in queue.items():
            items = outbound[place][link]
            if done < len(items) and held[place].get(items[done], now) < now:
                target = {"x": place ^ 1, "y": place ^ 2}.get(link, place)
                landed.append((target, inbound[target][link][done]))
                queue[place, link] = done + 1
        for target, item in landed:
            held[target][item] = now
            arrivals[target].append((now, item))
    for events in arrivals:
        events.sort(key=lambda event: (event[0], event[1][0] != 0))
    return outbound, arrivals, now


OUTBOUND, ARRIVALS, STEPS = zip(plan(OUTER_IN), plan(LIFTED_IN))


def shift_of(place, item):
    plane, chip, _ = item
    return PLANE * plane + chip - place


def chunk_order(place):
    ready = [{0: 0}, {0: 0}]
    for kind in range(2):
        for now, item in ARRIVALS[kind][place]:
            ready[kind][shift_of(place, item)] = now
    first = [0, (place ^ 1) - place, (place ^ 2) - place, -PLANE, PLANE]
    rest = sorted((ready[1][delta], now, delta) for delta, now in ready[0].items() if delta not in first)
    order = first + [delta for _, _, delta in rest]
    return order, [(ready[0][delta], ready[1][delta]) for delta in order]


def reduce_blocks(diag, bases, bases_t, work, low_corner):
    per_device, leaf_rows = bases.shape[0], bases.shape[1]
    red = leaf_rows - RANK
    row_id = lax.broadcasted_iota(jnp.int32, (red, red), 0)
    col_id = lax.broadcasted_iota(jnp.int32, (red, red), 1)
    for leaf in range(per_device):
        basis = bases[leaf]
        basis_t = basis.T
        bases_t[leaf] = basis_t
        half = matmul(basis_t, diag[leaf]).astype(jnp.bfloat16)
        dense = matmul(half, basis)
        top = dense[:red, :red]
        work[leaf, :, :red] = 0.5 * (top + top.T)
        work[leaf, :, red : red + RANK] = dense[:red, red:]
        work[leaf, :, red + RANK :] = (row_id == col_id).astype(jnp.float32)
        low_corner[leaf] = dense[red:, red:]


def eliminate(bases, lifted, turned, work, rows, serve):
    per_device, red = work.shape[0], work.shape[1]
    tiles = work.shape[2] // LANES
    row_id = lax.broadcasted_iota(jnp.int32, (red, red), 0)
    col_id = lax.broadcasted_iota(jnp.int32, (red, red), 1)
    sub = lax.broadcasted_iota(jnp.int32, (GROUP, LANES), 0)
    groups = PANEL // GROUP
    leaves = range(per_device)
    for start in range(0, red, PANEL):
        strips = [
            [
                [
                    work[leaf, pl.ds(start + GROUP * v, GROUP), pl.ds(LANES * t, LANES)]
                    for t in range(tiles)
                ]
                for v in range(groups)
            ]
            for leaf in leaves
        ]
        for g in range(groups):
            first = start + GROUP * g
            columns = [
                {
                    v: [
                        jnp.broadcast_to(strips[leaf][v][0][:, first + c : first + c + 1], (GROUP, LANES))
                        for c in range(GROUP)
                    ]
                    for v in range(g, groups)
                }
                for leaf in leaves
            ]
            for r in range(GROUP):
                for leaf in leaves:
                    cols, strip = columns[leaf], strips[leaf]
                    inverse = 1.0 / cols[g][r][r : r + 1]
                    heads = [cols[g][c][r : r + 1] for c in range(GROUP)]
                    lines = [strip[g][t][r : r + 1] for t in range(tiles)]
                    for v in range(g, groups):
                        ratio = cols[v][r] * inverse
                        if v == g:
                            ratio = jnp.where(sub > r, ratio, 0.0)
                        for c in range(r + 1, GROUP):
                            cols[v][c] = cols[v][c] - ratio * heads[c]
                        for t in range(tiles):
                            strip[v][t] = strip[v][t] - ratio * lines[t]
            for leaf in leaves:
                pivots = columns[leaf][g][0]
                for r in range(1, GROUP):
                    pivots = jnp.where(sub == r, columns[leaf][g][r], pivots)
                scale = 1.0 / jnp.sqrt(pivots)
                for t in range(tiles):
                    here = (leaf, pl.ds(first, GROUP), pl.ds(LANES * t, LANES))
                    rows[here] = strips[leaf][g][t] * scale
        if start + PANEL < red:
            for leaf in leaves:
                strip = rows[leaf, start : start + PANEL, :]
                work[leaf] = work[leaf] - matmul_t(strip[:, :red], strip, highest)
        serve(start // PANEL)
    for leaf in range(per_device):
        solved = rows[leaf, :, red : red + RANK]
        inverse = jnp.where(col_id <= row_id, rows[leaf, :, red + RANK :], 0.0)
        shift = matmul_t(inverse, solved, highest).astype(jnp.bfloat16)
        lifted[leaf] = matmul(bases[leaf, :, :red], shift).astype(jnp.bfloat16)
        back = -shift.astype(jnp.float32).T
        turned[leaf, :, :red] = back.astype(jnp.bfloat16)
        turned[leaf, :, red:] = back.astype(jnp.bfloat16)


def finish_factor(factor, panel, skeleton, rows, low_corner):
    per_device, red = rows.shape[0], rows.shape[1]
    row_id = lax.broadcasted_iota(jnp.int32, (red, red), 0)
    col_id = lax.broadcasted_iota(jnp.int32, (red, red), 1)
    for leaf in range(per_device):
        solved = rows[leaf, :, red : red + RANK]
        panel[leaf] = solved
        skeleton[leaf] = low_corner[leaf] - matmul_t(solved, solved, highest)
        upper = jnp.where(col_id >= row_id, rows[leaf, :, :red], 0.0)
        factor[leaf] = upper.T


def split(values):
    high = values.astype(jnp.bfloat16)
    return high, (values - high.astype(jnp.float32)).astype(jnp.bfloat16)


def level_kernel(
    count,
    parents,
    targets,
    nbrs,
    diag,
    bases,
    near,
    factor,
    panel,
    blocks,
    landed,
    win_outer,
    win_lifted,
    bases_in,
    diag_in,
    nbrs_in,
    low_corner,
    skeleton,
    turned,
    bases_t,
    work,
    rows,
    near_in,
    halves,
    diagonal,
    send,
    recv,
    pass_send,
    pass_recv,
    in_sem,
    near_sem,
    row_send,
    row_recv,
    found,
    lookup,
    found_sem,
):
    per_device, slots = near_in.shape[0], near_in.shape[1]
    red = rows.shape[1]
    total = count // 2
    me = lax.axis_index("leaf")
    core, chip = me % 2, me // 2
    sibling = me + 1 - 2 * core
    place = chip % PLANE
    size = CHILDREN // per_device
    seat = me % size
    across = me + 2 * (1 - 2 * (place % 2))
    along = me + 4 * (1 - 2 * (place // 2))
    device = {"x": across, "y": along, "up": me + 2 * PLANE, "down": me - 2 * PLANE}
    present = {"up": chip + PLANE < total, "down": chip - PLANE >= 0}
    far = across + 1 - 2 * core

    fetches = [
        pltpu.make_async_copy(near.at[leaf], near_in.at[leaf], near_sem.at[leaf])
        for leaf in range(per_device)
    ]
    here = 2 * PLANE + core
    inputs = [
        pltpu.make_async_copy(source, target, in_sem.at[n])
        for n, (source, target) in enumerate(
            (
                (nbrs, nbrs_in),
                (bases.at[:, :, pl.ds(red, RANK)], win_outer.at[here]),
                (bases, bases_in),
                (diag, diag_in),
            )
        )
    ]
    for copy in inputs + fetches:
        copy.start()

    barrier = pltpu.get_barrier_semaphore()
    for other in (sibling, across, along, far):
        pl.semaphore_signal(barrier, inc=1, device_id=(other,), device_id_type=MESH)
    peers = jnp.int32(4)
    for link in ("up", "down"):

        @pl.when(present[link])
        def _(link=link):
            pl.semaphore_signal(barrier, inc=1, device_id=(device[link],), device_id_type=MESH)

        peers = peers + present[link].astype(jnp.int32)

    windows = (win_outer, win_lifted)

    def exists(delta):
        return (chip + delta >= 0) & (chip + delta < total)

    def slot_of(delta, holder):
        return 2 * (PLANE + delta) + holder

    def block_of(kind, delta, holder, leaf):
        block = windows[kind].at[slot_of(delta, holder)]
        return block if leaf is None else block.at[leaf]

    def hop(kind, at, link, order):
        item = OUTBOUND[kind][at][link][order]
        delta, leaf = shift_of(at, item), item[2]
        moved = {"x": at - (at ^ 1), "y": at - (at ^ 2), "up": -PLANE, "down": PLANE}[link]
        return pltpu.make_async_remote_copy(
            src_ref=block_of(kind, delta, core, leaf),
            dst_ref=block_of(kind, delta + moved, core, leaf),
            send_sem=send.at[kind, LINKS.index(link), order],
            recv_sem=recv.at[kind, PLANE + delta + moved, leaf or 0],
            device_id=(device[link],),
            device_id_type=MESH,
        )

    def arrival(kind, delta, leaf):
        there = block_of(kind, delta, core, leaf)
        return pltpu.make_async_remote_copy(
            src_ref=there,
            dst_ref=there,
            send_sem=send.at[kind, 0, 0],
            recv_sem=recv.at[kind, PLANE + delta, leaf or 0],
            device_id=(sibling,),
            device_id_type=MESH,
        )

    def relay(kind, delta, leaf):
        there = block_of(kind, delta, core, leaf)
        return pltpu.make_async_remote_copy(
            src_ref=there,
            dst_ref=there,
            send_sem=pass_send.at[kind, PLANE + delta, leaf or 0],
            recv_sem=pass_recv.at[kind, PLANE + delta, leaf or 0],
            device_id=(sibling,),
            device_id_type=MESH,
        )

    def relayed(kind, delta, leaf):
        there = block_of(kind, delta, 1 - core, leaf)
        return pltpu.make_async_remote_copy(
            src_ref=there,
            dst_ref=there,
            send_sem=pass_send.at[kind, PLANE + delta, leaf or 0],
            recv_sem=pass_recv.at[kind, PLANE + delta, leaf or 0],
            device_id=(sibling,),
            device_id_type=MESH,
        )

    def parts(kind):
        return (None,) if kind else range(per_device)

    def on_links(kind, at, item, act):
        for link in LINKS:
            for order, entry in enumerate(OUTBOUND[kind][at][link]):
                if entry == item:
                    if link in present:
                        pl.when(present[link])(lambda: act(hop(kind, at, link, order)))
                    else:
                        act(hop(kind, at, link, order))

    def start(copy):
        copy.start()

    def stop(copy):
        copy.wait_send()

    def by_place(act):
        for at in range(PLANE):
            pl.when(place == at)(lambda: act(at))

    def dispatch(kind, leaf):
        by_place(lambda at: on_links(kind, at, (0, at, leaf), start))
        relay(kind, 0, leaf).start()

    def serve(kind, step):
        def act(at):
            for now, item in ARRIVALS[kind][at]:
                if now == step:
                    delta, leaf = shift_of(at, item), item[2]

                    def one():
                        arrival(kind, delta, leaf).wait_recv()
                        on_links(kind, at, item, start)
                        relay(kind, delta, leaf).start()

                    if item[0] == 0:
                        one()
                    else:
                        pl.when(exists(delta))(one)

        by_place(act)

    def finish(kind):
        def act(at):
            for leaf in parts(kind):
                on_links(kind, at, (0, at, leaf), stop)
            for _, item in ARRIVALS[kind][at]:
                delta, leaf = shift_of(at, item), item[2]

                def one():
                    on_links(kind, at, item, stop)
                    relay(kind, delta, leaf).wait_send()

                if item[0] == 0:
                    one()
                else:
                    pl.when(exists(delta))(one)

        by_place(act)
        for leaf in parts(kind):
            relay(kind, 0, leaf).wait_send()

    number = me * per_device
    parent = number // CHILDREN
    low = jnp.clip(parent - targets // 2, 0, parents - targets)
    home = parent - low
    inputs[1].wait()
    pl.semaphore_wait(barrier, peers)
    dispatch(0, 0)
    for copy in inputs[2:]:
        copy.wait()
    reduce_blocks(diag_in, bases_in, bases_t, work, low_corner)

    def clear():
        for row in range(targets):

            @pl.when((low + row < parent - 1) | (low + row > parent + 1))
            def _(row=row):
                blocks[:, row] = jnp.zeros_like(blocks[:, row])

        halves[:, slots] = jnp.zeros_like(halves[:, slots])

    reach = found.shape[1]
    table = pltpu.make_async_copy(found, lookup, found_sem)

    def look_up():
        offset = lax.broadcasted_iota(jnp.int32, (reach, slots), 0) - reach // 2
        order = lax.broadcasted_iota(jnp.int32, (reach, slots), 1)
        inputs[0].wait()
        for leaf in range(per_device):
            away = offset + number + leaf
            hit = (nbrs_in[leaf : leaf + 1, :] == away) & (away >= 0)
            slot = jnp.max(jnp.where(hit, order, -1), axis=1, keepdims=True)
            found[leaf] = jnp.broadcast_to(jnp.where(slot < 0, slots, slot), found.shape[1:])
        table.start()

    unroll = max(n for n in range(1, 14) if slots % n == 0)

    def project(turn):
        for k in range(unroll):
            n = turn * unroll + k
            for leaf in range(per_device):
                halves[leaf, n] = matmul(bases_t[leaf], near_in[leaf, n]).astype(jnp.bfloat16)

    orders = [chunk_order(at) for at in range(PLANE)]
    chunks = len(orders[0][0])

    def pick(values):
        chosen = jnp.int32(values[0])
        for at in range(1, PLANE):
            chosen = jnp.where(place == at, jnp.int32(values[at]), chosen)
        return chosen

    deltas = [pick([order[0][turn] for order in orders]) for turn in range(chunks)]

    def pairs_of(turn):
        delta = deltas[turn]
        for holder in range(2):
            for leaf in range(per_device):
                other = ((chip + delta) * 2 + holder) * per_device + leaf
                column = pl.multiple_of((other % CHILDREN) * RANK, RANK)
                yield holder, leaf, slot_of(delta, holder), other, other // CHILDREN - low, column

    def keep(turn, values):
        for (other, row, column, mine), act in values:
            if turn in (3, 4):
                apart = other - number - mine
                pl.when((apart <= REACH) & (apart >= -REACH))(lambda: act(row, column, mine))
            else:
                act(row, column, mine)

    def slot_for(other, mine):
        return lookup[mine, other - number - mine + reach // 2, 0]

    def first_half(turn):
        for leaf in parts(0):
            relayed(0, deltas[turn], leaf).wait_recv()
        coupled = {}
        targets_of = {}
        for holder, leaf, slot, other, row, column in pairs_of(turn):
            left = [halves[mine, slot_for(other, mine)] for mine in range(per_device)]
            both = matmul(jnp.concatenate(left, axis=0), win_outer[slot, leaf])
            for mine in range(per_device):
                targets_of[holder, leaf, mine] = (other, row, column, mine)
                part = both[mine * 2 * RANK : (mine + 1) * 2 * RANK]
                coupled[holder, leaf, mine] = (split(part[:red]), part[red:])
        kept = []
        for holder in range(2):
            for mine in range(per_device):
                tall = [
                    jnp.concatenate(coupled[holder, leaf, mine][0], axis=0)
                    for leaf in range(per_device)
                ]
                moved = matmul(turned[mine], jnp.concatenate(tall, axis=1))
                for leaf in range(per_device):
                    value = coupled[holder, leaf, mine][1] + moved[:, leaf * RANK : (leaf + 1) * RANK]

                    def act(row, column, mine, value=value):
                        blocks[mine, row, :, pl.ds(column, RANK)] = value

                    kept.append((targets_of[holder, leaf, mine], act))
        keep(turn, kept)

    def second_half(turn):
        for leaf in parts(1):
            relayed(1, deltas[turn], leaf).wait_recv()
        kept = []
        for holder, leaf, slot, other, row, column in pairs_of(turn):
            left = [halves[mine, slot_for(other, mine), red:] for mine in range(per_device)]
            both = matmul(jnp.concatenate(left, axis=0), win_lifted[slot, leaf])
            for mine in range(per_device):
                value = both[mine * RANK : (mine + 1) * RANK]

                def act(row, column, mine, value=value):
                    spot = blocks[mine, row, :, pl.ds(column, RANK)]
                    blocks[mine, row, :, pl.ds(column, RANK)] = spot - value

                kept.append(((other, row, column, mine), act))
        keep(turn, kept)

    def run(half, turn):
        pl.when(exists(deltas[turn]))(lambda: half(turn))

    def row_copy(t):
        other = (seat + t) % size
        width = per_device * RANK
        return pltpu.make_async_remote_copy(
            src_ref=diagonal.at[:, :, pl.ds(pl.multiple_of(other * width, 128), width)],
            dst_ref=landed.at[size - t],
            send_sem=row_send.at[t],
            recv_sem=row_recv.at[size - t],
            device_id=(me - seat + other,),
            device_id_type=MESH,
        )

    def send_rows():
        for leaf in range(per_device):
            column = pl.multiple_of(((number + leaf) % CHILDREN) * RANK, RANK)
            blocks[leaf, home, :, pl.ds(column, RANK)] = skeleton[leaf]
        for leaf in range(per_device):
            diagonal[leaf] = blocks[leaf, home].astype(jnp.bfloat16)
        for t in range(1, size):
            row_copy(t).start()

    def wait_near():
        for copy in fetches:
            copy.wait()
        table.wait()

    def between(panel_done):
        pass
        if panel_done == 0:
            dispatch(0, 1)
        if panel_done == 2:
            serve(0, 1)

    eliminate(bases_in, win_lifted.at[here], turned, work, rows, between)
    dispatch(1, None)
    finish_factor(factor, panel, skeleton, rows, low_corner)
    clear()
    look_up()
    wait_near()
    serve(0, 2)
    project(0)
    project(1)
    run(first_half, 0)
    run(first_half, 1)
    serve(1, 1)
    serve(0, 3)
    run(second_half, 0)
    run(second_half, 1)
    run(first_half, 2)
    run(first_half, 3)
    run(first_half, 4)
    send_rows()
    serve(0, 4)
    serve(1, 2)
    run(second_half, 2)
    run(second_half, 3)
    run(second_half, 4)
    run(first_half, 5)
    run(first_half, 6)
    serve(0, 5)
    run(first_half, 7)
    run(first_half, 8)
    serve(1, 3)
    run(second_half, 5)
    run(second_half, 6)
    run(second_half, 7)
    run(second_half, 8)
    finish(0)
    finish(1)
    for t in range(1, size):
        row_copy(size - t).wait_recv()
    for t in range(1, size):
        row_copy(t).wait_send()


def place_kernel(
    parents, factor, panel, blocks, landed, factor_out, panel_out, merged, block_out, block, sems
):
    per_device, targets = blocks.shape[0], blocks.shape[1]
    size = landed.shape[0]
    width = per_device * RANK
    me = lax.axis_index("leaf")
    seat = me % size
    parent = me * per_device // CHILDREN
    low = jnp.clip(parent - targets // 2, 0, parents.shape[0] - targets)
    copies = []

    def put(source, target):
        copy = pltpu.make_async_copy(source, target, sems.at[len(copies)])
        copy.start()
        copies.append(copy)

    for q in range(targets):
        row = parents[parent, q] - low
        for leaf in range(per_device):
            put(blocks.at[leaf, row], merged.at[leaf, q])
    put(factor, factor_out)
    put(panel, panel_out)
    for t in range(size):
        columns = pl.ds(pl.multiple_of(((seat + t) % size) * width, 128), width)
        mine = blocks[:, parent - low, :, columns].reshape(width, width)
        if t == 0:
            theirs = mine
        else:
            theirs = landed[t].reshape(width, width).astype(jnp.float32)
        block[:, columns] = 0.5 * (mine + theirs.T)
        put(block.at[:, columns], block_out.at[:, columns])
    for copy in copies:
        copy.wait()


def local(count, near_blocks, diag_blocks, bases, leaf_nbrs, parent_nbrs):
    per_device, leaf_rows = bases.shape[0], bases.shape[1]
    red = leaf_rows - RANK
    slots = near_blocks.shape[1]
    parents, targets = parent_nbrs.shape
    assert per_device == 2 and REACH == 4 * PLANE
    vmem = pl.BlockSpec(memory_space=pltpu.VMEM)
    smem = pl.BlockSpec(memory_space=pltpu.SMEM)
    hbm = pl.BlockSpec(memory_space=pltpu.HBM)
    f32, bf16 = jnp.float32, jnp.bfloat16

    def in_hbm(array):
        return pltpu.with_memory_space_constraint(array, pltpu.HBM)

    def out(shape, dtype):
        return jax.ShapeDtypeStruct(shape, dtype)

    reach = 2 * (REACH + CHILDREN)
    size = CHILDREN // per_device
    width = per_device * RANK
    window = 2 * (2 * PLANE + 1)
    links = max(len(out_[link]) for kind in OUTBOUND for out_ in kind for link in LINKS)
    sems = pltpu.SemaphoreType.DMA
    factor, panel, blocks, landed = pl.pallas_call(
        functools.partial(level_kernel, count, parents, targets),
        out_shape=(
            out((per_device, red, red), f32),
            out((per_device, red, RANK), f32),
            out((per_device, targets, RANK, CHILDREN * RANK), f32),
            out((size, per_device, RANK, width), bf16),
        ),
        in_specs=[hbm] * 4,
        out_specs=(vmem,) * 4,
        scratch_shapes=[
            pltpu.VMEM((window, per_device, leaf_rows, RANK), bf16),
            pltpu.VMEM((window, per_device, leaf_rows, RANK), bf16),
            pltpu.VMEM(bases.shape, bf16),
            pltpu.VMEM(diag_blocks.shape, bf16),
            pltpu.VMEM(leaf_nbrs.shape, jnp.int32),
            pltpu.VMEM((per_device, RANK, RANK), f32),
            pltpu.VMEM((per_device, RANK, RANK), f32),
            pltpu.VMEM((per_device, RANK, 2 * red), bf16),
            pltpu.VMEM(bases.shape, bf16),
            pltpu.VMEM((per_device, red, 2 * red + RANK), f32),
            pltpu.VMEM((per_device, red, 2 * red + RANK), f32),
            pltpu.VMEM(near_blocks.shape, bf16),
            pltpu.VMEM((per_device, slots + 1) + near_blocks.shape[2:], bf16),
            pltpu.VMEM((per_device, RANK, CHILDREN * RANK), bf16),
            sems((2, len(LINKS), links)),
            sems((2, 2 * PLANE + 1, per_device)),
            sems((2, 2 * PLANE + 1, per_device)),
            sems((2, 2 * PLANE + 1, per_device)),
            sems((4,)),
            sems((per_device,)),
            sems((size,)),
            sems((size,)),
            pltpu.VMEM((per_device, reach, 128), jnp.int32),
            pltpu.SMEM((per_device, reach, 128), jnp.int32),
            sems(()),
        ],
        compiler_params=pltpu.CompilerParams(
            collective_id=0, has_side_effects=True, vmem_limit_bytes=46_500_000
        ),
        name="level",
    )(*(in_hbm(array) for array in (leaf_nbrs, diag_blocks, bases, near_blocks)))

    return pl.pallas_call(
        place_kernel,
        out_shape=(
            out((per_device, red, red), f32),
            out((per_device, red, RANK), f32),
            out((per_device, targets, RANK, CHILDREN * RANK), f32),
            out((width, CHILDREN * RANK), f32),
        ),
        in_specs=[smem, vmem, vmem, vmem, vmem],
        out_specs=(hbm,) * 4,
        scratch_shapes=[
            pltpu.VMEM((width, CHILDREN * RANK), f32),
            sems((targets * per_device + 2 + size,)),
        ],
        compiler_params=pltpu.CompilerParams(vmem_limit_bytes=16_000_000),
        name="place",
    )(parent_nbrs, factor, panel, blocks, landed)


def solution(mesh):
    count = mesh.shape["leaf"]
    in_specs = (
        P("leaf", None, None, None),
        P("leaf", None, None),
        P("leaf", None, None),
        P("leaf", None),
        P(),
    )
    out_specs = (
        P("leaf", None, None),
        P("leaf", None, None),
        P("leaf", None, None, None),
        P("leaf", None),
    )
    return jax.shard_map(
        functools.partial(local, count),
        mesh=mesh,
        in_specs=in_specs,
        out_specs=out_specs,
        check_vma=False,
    )
```
